32 devices in a mesh: tile: 8 (over y, x, core), fsdp: 4 (over z).
Axes of the slice: x: 2, y: 2, z: 4, core: 2. Of those that a mesh axis runs over, the one named last changes fastest.
Arguments:
- tiles_in: bfloat16 [64, 32, 32, 256], P(('tile', 'fsdp')), may hold values from -6 to 6
- first_weight: bfloat16 [512, 2304], P('fsdp'), may hold values from -0.125 to 0.125
- first_bias: float32 [512], replicated, may hold values from -3 to 3
- second_weight: bfloat16 [512, 4608], P('fsdp'), may hold values from -0.09375 to 0.09375
- second_bias: float32 [512], replicated, may hold values from -3 to 3
- side_links: int32 [64, 4, 3], P(('tile', 'fsdp')), may hold values from 0 to 63, as said below
- corner_links: int32 [64, 4, 3], P(('tile', 'fsdp')), may hold values from 0 to 63, as said below
Outputs:
- pooled: bfloat16 [64, 16, 16, 512], P(('tile', 'fsdp'))
The draws below stay inside these ranges and needn't reach their ends.
Inputs may be any that keep to these rules, and one draw needn't show every extreme that they name: `side_links`: the tile across side s (0 north, 1 east, 2 south, 3 west) of a tile lies on the device one step in that direction, with wrap, in the grid whose rows are the tile index and whose columns are the fsdp index; a tile id g lies on the device numbered g // 2 with the fsdp index fastest. The second entry is a side 0..3, the third a flag 0 or 1. `corner_links`: the tile at corner c (0 north-west, 1 north-east, 2 south-east, 3 south-west) lies on the diagonal device in that direction, with wrap, in the same grid; the second entry is a corner 0..3, the third is 1 where four or five tiles meet and 0 where three meet.
All inputs are finite; a program needn't handle non-finite values.
Results may differ from the reference program's by a relative error of at most 0.0031.
Values may be sent and summed in bfloat16 or wider, within the bound.
No kernel may reach another device: no remote copies, remote signals or barrier semaphores. Data moves between devices by JAX's collectives and lax.ppermute only.
A program may use at most 384 MiB of HBM per device.

```python
import jax
import jax.numpy as jnp
from jax import lax

CIN = 256
COUT = 512
P_SIZE = 32
TILE_DEV = 2
TILES = 64
N_TILE = 8
N_FSDP = 4


def link_table(key, row_steps, col_steps, flag_top):
    tile_ids = jnp.arange(TILES, dtype=jnp.int32)
    device_id = tile_ids // TILE_DEV
    grid_row = device_id // N_FSDP
    grid_col = device_id % N_FSDP
    key_local, key_pick, key_flag = jax.random.split(key, 3)
    near_row = (grid_row[:, None] + jnp.array(row_steps, jnp.int32)[None, :]) % N_TILE
    near_col = (grid_col[:, None] + jnp.array(col_steps, jnp.int32)[None, :]) % N_FSDP
    local_tile = jax.random.randint(key_local, (TILES, 4), 0, TILE_DEV, dtype=jnp.int32)
    near_ids = (near_row * N_FSDP + near_col) * TILE_DEV + local_tile
    pick_index = jax.random.randint(key_pick, (TILES, 4), 0, 4, dtype=jnp.int32)
    flag_value = jax.random.randint(key_flag, (TILES, 4), 0, flag_top, dtype=jnp.int32)
    return (near_ids, pick_index, flag_value)


def draw_side_links(key, part):
    near_ids, pick_index, flag_value = link_table(jax.random.fold_in(key, 11), [-1, 0, 1, 0], [0, 1, 0, -1], 2)
    return jnp.stack([near_ids, pick_index, flag_value], axis=-1).astype(jnp.int32)


def draw_corner_links(key, part):
    near_ids, pick_index, flag_value = link_table(jax.random.fold_in(key, 23), [-1, -1, 1, 1], [-1, 1, 1, -1], 4)
    live_flag = jnp.where(flag_value > 0, 1, 0).astype(jnp.int32)
    return jnp.stack([near_ids, pick_index, live_flag], axis=-1).astype(jnp.int32)


def level_of(own_key, shape, cuts, least, largest):
    loudness = 1.0
    for dim, blocks in cuts:
        heights = jax.random.uniform(jax.random.fold_in(jax.random.fold_in(own_key, 6), dim), (blocks,), jnp.float32, least / len(cuts), largest / len(cuts))
        loudness = loudness * jnp.repeat(jnp.exp(heights), shape[dim] // blocks).reshape((-1,) + (1,) * (len(shape) - 1 - dim))
    return loudness


def gaussian(key, dims, spread, limit, shards=(), held_as=jnp.bfloat16):
    loudness = level_of(key, dims, shards, -0.22, 0.18) if shards else 1.0
    result = jax.random.normal(key, dims, jnp.float32) * spread * loudness
    return jnp.minimum(jnp.maximum(result, -limit), limit).astype(held_as)


def setup_inputs(seed: int = 0) -> dict:
    key_list = jax.random.split(jax.random.key(seed), 8)
    return {
        "tiles_in": gaussian(key_list[0], (TILES, P_SIZE, P_SIZE, CIN), 1.0, 6.0, ((0, 32),)),
        "first_weight": gaussian(key_list[1], (COUT, 9 * CIN), (9 * CIN) ** -0.5, 0.125, ((0, 4),)),
        "first_bias": gaussian(key_list[2], (COUT,), 0.5, 3.0, (), jnp.float32),
        "second_weight": gaussian(key_list[3], (COUT, 9 * COUT), (9 * COUT) ** -0.5, 0.09375, ((0, 4),)),
        "second_bias": gaussian(key_list[4], (COUT,), 0.5, 3.0, (), jnp.float32),
        "side_links": draw_side_links(jax.random.fold_in(key_list[7], 71), 0),
        "corner_links": draw_corner_links(jax.random.fold_in(key_list[7], 71), 0),
    }


def border_parts(field):
    strips = jnp.stack([field[:, 0, :, :], field[:, :, -1, :], field[:, -1, ::-1, :], field[:, ::-1, 0, :]], axis=1)
    corners = jnp.stack([field[:, 0, 0, :], field[:, 0, -1, :], field[:, -1, -1, :], field[:, -1, 0, :]], axis=1)
    return strips, corners


def assemble(field, side_halo, corner_halo):
    upper_row = jnp.concatenate([corner_halo[:, 0:1], side_halo[:, 0], corner_halo[:, 1:2]], axis=1)
    bottom = jnp.concatenate([corner_halo[:, 3:4], side_halo[:, 2, ::-1], corner_halo[:, 2:3]], axis=1)
    middle = jnp.concatenate([side_halo[:, 3, ::-1, None, :], field, side_halo[:, 1, :, None, :]], axis=2)
    return jnp.concatenate([upper_row[:, None], middle, bottom[:, None]], axis=1)


def surround(field, side_links, corner_links):
    strips, corners = border_parts(field)
    chosen = strips[side_links[..., 0], side_links[..., 1]]
    chosen = jnp.where(side_links[..., 2][..., None, None] == 1, chosen, chosen[:, :, ::-1])
    corner_halo = corners[corner_links[..., 0], corner_links[..., 1]]
    corner_halo = jnp.where(corner_links[..., 2][..., None] == 1, corner_halo, jnp.zeros_like(corner_halo))
    return assemble(field, chosen, corner_halo)


def convolve(padded, weight):
    edge_len = padded.shape[0] - 2
    channels = padded.shape[2]
    running = jnp.zeros((edge_len * edge_len, weight.shape[0]), jnp.float32)
    for row_step in range(3):
        for col_step in range(3):
            tap_index = 3 * row_step + col_step
            window = padded[row_step:row_step + edge_len, col_step:col_step + edge_len, :].reshape(edge_len * edge_len, channels)
            tap_weight = weight[:, tap_index * channels:(tap_index + 1) * channels]
            running = running + jnp.dot(window.astype(jnp.float32), tap_weight.astype(jnp.float32).T)
    return running.reshape(edge_len, edge_len, weight.shape[0])


def reference(tiles_in, first_weight, first_bias, second_weight, second_bias, side_links, corner_links):
    padded_first = surround(tiles_in, side_links, corner_links)

    def first_tile(padded):
        return jax.nn.gelu(convolve(padded, first_weight) + first_bias, approximate=False).astype(jnp.bfloat16)

    hidden = lax.map(first_tile, padded_first)
    padded_second = surround(hidden, side_links, corner_links)

    def second_tile(padded):
        act_full = jax.nn.gelu(convolve(padded, second_weight) + second_bias, approximate=False)
        half = act_full.shape[0] // 2
        return act_full.reshape(half, 2, half, 2, act_full.shape[2]).mean(axis=(1, 3)).astype(jnp.bfloat16)

    return lax.map(second_tile, padded_second)
```

```python
import jax
import jax.numpy as jnp
from jax import lax
from jax.sharding import PartitionSpec as P


AXES = ("tile", "fsdp")


def move(x, target):
    rows, cols = (lax.axis_size("tile"), lax.axis_size("fsdp"))
    pairs = []
    for t in range(rows):
        for f in range(cols):
            there_t, there_f = target(t, f)
            pairs.append((t * cols + f, (there_t % rows) * cols + there_f % cols))
    return lax.ppermute(x, AXES, pairs)


def shift(x, rows, cols):
    return move(x, lambda t, f: (t + rows, f + cols))


def gather_rows(weight):
    rows, cols = (lax.axis_size("tile"), lax.axis_size("fsdp"))
    tall = rows // 4
    share = weight.shape[0] // rows
    width = weight.shape[1]
    parts = weight.reshape(rows, share, width)
    mine = lax.dynamic_index_in_dim(parts, lax.axis_index("tile"), 0, keepdims=True)
    unit = jnp.concatenate([shift(mine, 0, k) for k in range(1, cols)], axis=0)
    near = [unit]
    for step in range(1, 2 * tall):
        dy, dx = divmod(step, 2)
        near.append(
            move(unit, lambda t, f: (((t // 4 + dy) % tall) * 4 + ((t // 2 % 2) ^ dx) * 2 + t % 2, f))
        )
    near = jnp.stack(near)
    other = move(near, lambda t, f: (t ^ 1, f))
    return jnp.stack([near, other])


def place(weight, pieces):
    rows, cols = (lax.axis_size("tile"), lax.axis_size("fsdp"))
    tall = rows // 4
    share, width = pieces.shape[3:]
    t, f = (lax.axis_index("tile"), lax.axis_index("fsdp"))
    pieces = pieces.reshape(2 * 2 * tall * (cols - 1), share, width)
    source_f = jnp.arange(cols)[:, None]
    source_t = jnp.arange(rows)[None, :]
    core = (source_t ^ t) & 1
    dx = ((source_t ^ t) >> 1) & 1
    dy = (t // 4 - source_t // 4) % tall
    hop = (f - source_f) % cols
    index = (core * 2 * tall + dy * 2 + dx) * (cols - 1) + hop - 1
    index = jnp.where(hop == 0, 0, index)
    whole = jnp.take(pieces, index.reshape(-1), axis=0).reshape(cols, rows * share, width)
    whole = lax.dynamic_update_index_in_dim(whole, weight, f, 0)
    return whole.reshape(-1, width)


def border_parts(field):
    strips = jnp.stack(
        [field[:, 0, :, :], field[:, :, -1, :], field[:, -1, ::-1, :], field[:, ::-1, 0, :]], axis=1
    )
    corners = jnp.stack(
        [field[:, 0, 0, :], field[:, 0, -1, :], field[:, -1, -1, :], field[:, -1, 0, :]], axis=1
    )
    return (strips, corners)


def assemble(field, side_halo, corner_halo):
    upper_row = jnp.concatenate([corner_halo[:, 0:1], side_halo[:, 0], corner_halo[:, 1:2]], axis=1)
    bottom = jnp.concatenate(
        [corner_halo[:, 3:4], side_halo[:, 2, ::-1], corner_halo[:, 2:3]], axis=1
    )
    middle = jnp.concatenate(
        [side_halo[:, 3, ::-1, None, :], field, side_halo[:, 1, :, None, :]], axis=2
    )
    return jnp.concatenate([upper_row[:, None], middle, bottom[:, None]], axis=1)


def halo(field, side_links, corner_links):
    per_device, edge_len, _, channels = field.shape
    strips, corners = border_parts(field)
    strips = strips.reshape(per_device * 4, edge_len, channels)
    corners = corners.reshape(per_device * 4, channels)
    bundle = jnp.concatenate([strips.reshape(-1, channels), corners], axis=0)
    north = shift(bundle, 1, 0)
    south = shift(bundle, -1, 0)
    cut = per_device * 4 * edge_len
    bundle = jnp.concatenate([bundle[:cut], north[cut:], south[cut:]], axis=0)
    west = shift(bundle, 0, 1)
    east = shift(bundle, 0, -1)
    step = per_device * 4
    sides = []
    for s, near in enumerate((north, east, south, west)):
        near = near[:cut].reshape(step, edge_len, channels)
        chosen = jnp.take(near, side_links[:, s, 0] % per_device * 4 + side_links[:, s, 1], axis=0)
        sides.append(jnp.where(side_links[:, s, 2, None, None] == 1, chosen, chosen[:, ::-1]))
    cells = []
    for c, (near, low) in enumerate(((west, 0), (east, 0), (east, step), (west, step))):
        near = near[cut + low : cut + low + step]
        chosen = jnp.take(near, corner_links[:, c, 0] % per_device * 4 + corner_links[:, c, 1], axis=0)
        cells.append(jnp.where(corner_links[:, c, 2, None] == 1, chosen, jnp.zeros_like(chosen)))
    return jnp.stack(sides, axis=1), jnp.stack(cells, axis=1)


def convolve(padded, weight_rows):
    edge_len = padded.shape[1] - 2
    channels = padded.shape[3]
    running = jnp.zeros((padded.shape[0], edge_len, edge_len, weight_rows.shape[0]), jnp.float32)
    for row_step in range(3):
        for col_step in range(3):
            tap_index = 3 * row_step + col_step
            window = padded[:, row_step : row_step + edge_len, col_step : col_step + edge_len, :]
            tap_weight = weight_rows[:, tap_index * channels : (tap_index + 1) * channels]
            running = running + lax.dot_general(
                window, tap_weight, (((3,), (1,)), ((), ())), preferred_element_type=jnp.float32
            )
    return running


def finish(pre_act, bias, width):
    act_full = jax.nn.gelu(pre_act + bias, approximate=False)
    half = act_full.shape[1] // 2
    pooled = act_full.reshape(act_full.shape[0], half, 2, half, 2, width).mean(axis=(2, 4))
    return pooled.astype(jnp.bfloat16)


def shards(
    tiles_in, first_weight, first_bias, second_weight, second_bias, side_links, corner_links
):
    first_pieces = gather_rows(first_weight)
    second_pieces = gather_rows(second_weight)
    padded_first = assemble(tiles_in, *halo(tiles_in, side_links, corner_links))
    pre_act = convolve(padded_first, place(first_weight, first_pieces)) + first_bias
    hidden = jax.nn.gelu(pre_act, approximate=False).astype(jnp.bfloat16)
    padded_second = assemble(hidden, *halo(hidden, side_links, corner_links))
    weight_rows = place(second_weight, second_pieces)
    return finish(convolve(padded_second, weight_rows), second_bias, weight_rows.shape[0])


def solution(mesh):
    placed = (
        P(AXES, None, None, None),
        P("fsdp", None),
        P(),
        P("fsdp", None),
        P(),
        P(AXES, None, None),
        P(AXES, None, None),
    )
    return jax.shard_map(
        shards,
        mesh=mesh,
        in_specs=placed,
        out_specs=P(AXES, None, None, None),
        check_vma=False,
    )
```

```python
import functools

import jax
import jax.numpy as jnp
from jax import lax
from jax.experimental import pallas as pl
from jax.experimental.pallas import tpu as pltpu
from jax.sharding import PartitionSpec as P


AXES = ("tile", "fsdp")
PAD = 16


def move(x, target):
    rows, cols = (lax.axis_size("tile"), lax.axis_size("fsdp"))
    pairs = []
    for t in range(rows):
        for f in range(cols):
            there_t, there_f = target(t, f)
            pairs.append((t * cols + f, (there_t % rows) * cols + there_f % cols))
    return lax.ppermute(x, AXES, pairs)


def shift(x, rows, cols):
    return move(x, lambda t, f: (t + rows, f + cols))


def gather_rows(weight):
    rows, cols = (lax.axis_size("tile"), lax.axis_size("fsdp"))
    tall = rows // 4
    share = weight.shape[0] // rows
    width = weight.shape[1]
    parts = weight.reshape(rows, share, width)
    mine = lax.dynamic_index_in_dim(parts, lax.axis_index("tile"), 0, keepdims=True)
    unit = jnp.concatenate([shift(mine, 0, k) for k in range(1, cols)], axis=0)
    near = [unit]
    for step in range(1, 2 * tall):
        dy, dx = divmod(step, 2)
        near.append(
            move(unit, lambda t, f: (((t // 4 + dy) % tall) * 4 + ((t // 2 % 2) ^ dx) * 2 + t % 2, f))
        )
    near = jnp.stack(near)
    other = move(near, lambda t, f: (t ^ 1, f))
    return jnp.stack([near, other])


def place(weight, pieces):
    rows, cols = (lax.axis_size("tile"), lax.axis_size("fsdp"))
    tall = rows // 4
    share, width = pieces.shape[3:]
    t, f = (lax.axis_index("tile"), lax.axis_index("fsdp"))
    pieces = pieces.reshape(2 * 2 * tall * (cols - 1), share, width)
    source_f = jnp.arange(cols)[:, None]
    source_t = jnp.arange(rows)[None, :]
    core = (source_t ^ t) & 1
    dx = ((source_t ^ t) >> 1) & 1
    dy = (t // 4 - source_t // 4) % tall
    hop = (f - source_f) % cols
    index = (core * 2 * tall + dy * 2 + dx) * (cols - 1) + hop - 1
    index = jnp.where(hop == 0, 0, index)
    whole = jnp.take(pieces, index.reshape(-1), axis=0).reshape(cols, rows * share, width)
    whole = lax.dynamic_update_index_in_dim(whole, weight, f, 0)
    return whole.reshape(-1, width)


def gelu(x):
    return 0.5 * x * (1.0 + lax.erf(x * (0.5**0.5)))


def one_hot(rows, width, target):
    n = lax.broadcasted_iota(jnp.int32, (rows, width), 0)
    return jnp.where(lax.broadcasted_iota(jnp.int32, (rows, width), 1) == target(n), 1.0, 0.0).astype(
        jnp.bfloat16
    )


def select(picker, values):
    return jnp.dot(picker, values, preferred_element_type=jnp.float32)


def put_borders(bundle, tile, half, chunk, edge):
    rows = edge // 2
    sides = one_hot(
        edge, rows * edge, lambda n: jnp.where(n < rows, n * edge, (n - rows) * edge + edge - 1)
    )
    sides = select(sides, chunk).astype(jnp.bfloat16)
    start = tile * 4 * edge
    bundle[pl.ds(start + 3 * edge + half * rows, rows), :] = sides[:rows]
    bundle[pl.ds(start + edge + half * rows, rows), :] = sides[rows:]
    if half == 0:
        bundle[pl.ds(start, edge), :] = chunk[:edge]
    else:
        bundle[pl.ds(start + 2 * edge, edge), :] = chunk[-edge:]


def put_corners(bundle, tiles, edge):
    def source(n):
        corner = n & 3
        across = jnp.where((corner == 1) | (corner == 2), edge - 1, 0)
        return (n >> 2) * 4 * edge + jnp.where(corner >= 2, 2 * edge, 0) + across

    strips = tiles * 4 * edge
    cells = select(one_hot(PAD, strips, source), bundle[:strips, :])
    bundle[strips:, :] = cells.astype(jnp.bfloat16)


def borders_kernel(field, bundle):
    tiles, edge, _, channels = field.shape
    for tile in range(tiles):
        for half in range(2):
            rows = edge // 2
            chunk = field[tile, half * rows : (half + 1) * rows].reshape(rows * edge, channels)
            put_borders(bundle, tile, half, chunk, edge)
    put_corners(bundle, tiles, edge)


def borders(field):
    tiles, edge, _, channels = field.shape
    return pl.pallas_call(
        borders_kernel,
        out_shape=jax.ShapeDtypeStruct((tiles * 4 * edge + PAD, channels), jnp.bfloat16),
        name="borders",
    )(field)


def surround(field, near, side_links, corner_links, halos, wide):
    tiles, edge, _, channels = field.shape
    strips = tiles * 4 * edge
    column = lax.broadcasted_iota(jnp.int32, (edge, channels), 0)

    def put(tile, row, middle, before, after):
        spread = middle.astype(jnp.float32)
        left = jnp.where(column == 0, before, pltpu.roll(spread, 1, 0))
        right = jnp.where(column == edge - 1, after, pltpu.roll(spread, edge - 1, 0))
        wide[tile, row, :, :channels] = left.astype(jnp.bfloat16)
        wide[tile, row, :, channels : 2 * channels] = middle.astype(jnp.bfloat16)
        wide[tile, row, :, 2 * channels :] = right.astype(jnp.bfloat16)

    for tile in range(tiles):
        for side in range(4):
            link = (tile * 4 + side) * 3
            home = lax.rem(side_links[link], tiles) * 4 + side_links[link + 1]
            turns = (
                (1 if side >= 2 else 0)
                + jnp.where(side_links[link + 1] >= 2, 1, 0)
                + jnp.where(side_links[link + 2] == 1, 0, 1)
            )
            forward = lax.rem(turns, 2) == 0
            first = home * edge + jnp.where(forward, 0, edge - 1)
            step = jnp.where(forward, 1, -1)
            picker = one_hot(edge, strips, lambda n: first + step * n)
            halos[tile, side] = select(picker, near[side][:strips, :])
        cells = []
        for corner, (source, low) in enumerate(((3, 0), (1, 0), (1, PAD), (3, PAD))):
            link = (tile * 4 + corner) * 3
            pick = lax.rem(corner_links[link], tiles) * 4 + corner_links[link + 1]
            pick = jnp.where(corner_links[link + 2] == 1, pick, -1)
            picker = one_hot(8, PAD, lambda n: pick)
            cells.append(select(picker, near[source][strips + low : strips + low + PAD, :])[:1])
        put(tile, 0, halos[tile, 0], cells[0], cells[1])
        put(tile, edge + 1, halos[tile, 2], cells[3], cells[2])

        @pl.loop(0, edge // 4)
        def _(block):
            for offset in range(4):
                row = block * 4 + offset
                before = halos[tile, 3, pl.ds(row, 1), :]
                after = halos[tile, 1, pl.ds(row, 1), :]
                put(tile, row + 1, field[tile, row], before, after)


def fetch_weight(sources, whole, place_of, sems):
    copies = []
    if len(sources) == 1:
        copies.append(pltpu.make_async_copy(sources[0], whole, sems.at[0]))
    else:
        own, pieces = sources
        _, steps, hops, share, _ = pieces.shape
        cols = hops + 1
        rows = own.shape[0] // share
        t, f = (place_of[0], place_of[1])
        tall = steps // 2
        copies.append(
            pltpu.make_async_copy(
                own, whole.at[pl.ds(pl.multiple_of(f * rows * share, share), rows * share)], sems.at[0]
            )
        )
        for core in range(2):
            for step in range(steps):
                dy, dx = divmod(step, 2)
                far_y = lax.rem(t // 4 + tall - dy, tall)
                far_x = lax.rem(t // 2 + dx, 2)
                far = far_y * 4 + far_x * 2 + lax.rem(t + core, 2)
                for hop in range(1, cols):
                    far_f = lax.rem(f + cols - hop, cols)
                    start = pl.multiple_of((far_f * rows + far) * share, share)
                    copies.append(
                        pltpu.make_async_copy(
                            pieces.at[core, step, hop - 1], whole.at[pl.ds(start, share)], sems.at[len(copies)]
                        )
                    )
    for copy in copies:
        copy.start()
    return copies


def conv_kernel(count, pooling, *refs):
    place_of, side_links, corner_links, field, north, east, south, west, bias = refs[:9]
    sources = refs[9 : 9 + count]
    outs = refs[9 + count : -5]
    halos, wide, whole, sems, total = refs[-5:]
    tiles, edge, _, channels = field.shape
    copies = fetch_weight(sources, whole, place_of, sems)
    surround(field, (north, east, south, west), side_links, corner_links, halos, wide)
    for copy in copies:
        copy.wait()
    rows = edge // 2
    depth = 3 * channels
    for tile in range(tiles):
        for half in range(2):
            low = half * rows
            summed = bias[...]
            for tap in range(3):
                window = wide[tile, low + tap : low + tap + rows].reshape(rows * edge, depth)
                summed = summed + lax.dot_general(
                    window,
                    whole[:, tap * depth : (tap + 1) * depth],
                    (((1,), (1,)), ((), ())),
                    preferred_element_type=jnp.float32,
                )
            act = gelu(summed)
            if pooling:
                width = act.shape[1]
                act = act.reshape(rows // 2, 2, edge, width)
                act = (act[:, 0] + act[:, 1]).reshape(rows // 2 * edge, width)
                mean = []
                for lanes in range(0, width, 128):
                    total[...] = act[:, lanes : lanes + 128]
                    even = total[pl.ds(0, rows * edge // 4, stride=2), :]
                    odd = total[pl.ds(1, rows * edge // 4, stride=2), :]
                    mean.append(((even + odd) * 0.25).astype(jnp.bfloat16))
                mean = jnp.concatenate(mean, axis=1)
                outs[0][tile, low // 2 : (low + rows) // 2] = mean.reshape(rows // 2, edge // 2, width)
            else:
                hidden = act.astype(jnp.bfloat16)
                outs[0][tile, low : low + rows] = hidden.reshape(rows, edge, act.shape[1])
                put_borders(outs[1], tile, half, hidden, edge)
    if not pooling:
        put_corners(outs[1], tiles, edge)


def conv(field, near, place_of, side_links, corner_links, bias, sources, pooling):
    tiles, edge, _, channels = field.shape
    width = bias.shape[0]
    if pooling:
        outs = (jax.ShapeDtypeStruct((tiles, edge // 2, edge // 2, width), jnp.bfloat16),)
    else:
        outs = (
            jax.ShapeDtypeStruct((tiles, edge, edge, width), jnp.bfloat16),
            jax.ShapeDtypeStruct((tiles * 4 * edge + PAD, width), jnp.bfloat16),
        )
    vmem = pl.BlockSpec(memory_space=pltpu.VMEM)
    smem = pl.BlockSpec(memory_space=pltpu.SMEM)
    anywhere = pl.BlockSpec(memory_space=pl.ANY)
    copies = 1 if len(sources) == 1 else 1 + sources[1].shape[0] * sources[1].shape[1] * sources[1].shape[2]
    flops = 2 * tiles * edge * edge * 9 * channels * width
    return pl.pallas_call(
        functools.partial(conv_kernel, len(sources), pooling),
        out_shape=outs,
        in_specs=[smem] * 3 + [vmem] * 6 + [anywhere] * len(sources),
        out_specs=[vmem] * len(outs),
        scratch_shapes=[
            pltpu.VMEM((tiles, 4, edge, channels), jnp.float32),
            pltpu.VMEM((tiles, edge + 2, edge, 3 * channels), jnp.bfloat16),
            pltpu.VMEM((width, 9 * channels), jnp.bfloat16),
            pltpu.SemaphoreType.DMA((copies,)),
            pltpu.VMEM((edge * edge // 4, 128), jnp.float32),
        ],
        cost_estimate=pl.CostEstimate(flops=flops, bytes_accessed=8 << 20, transcendentals=0),
        name="second" if pooling else "first",
    )(
        place_of,
        side_links.reshape(-1),
        corner_links.reshape(-1),
        field,
        *near,
        bias.reshape(1, width),
        *sources,
    )


def exchange(bundle):
    north = shift(bundle, 1, 0)
    south = shift(bundle, -1, 0)
    strips = bundle.shape[0] - PAD
    bundle = jnp.concatenate([bundle[:strips], north[strips:], south[strips:]], axis=0)
    west = shift(bundle, 0, 1)
    east = shift(bundle, 0, -1)
    return north, east, south, west


def sources_of(weight):
    pieces = gather_rows(weight)
    if pieces.shape[3] % 16 == 0:
        return (weight, pieces)
    return (place(weight, pieces),)


def shards(
    tiles_in, first_weight, first_bias, second_weight, second_bias, side_links, corner_links
):
    place_of = jnp.stack([lax.axis_index("tile"), lax.axis_index("fsdp")])
    first = sources_of(first_weight)
    second = sources_of(second_weight)
    links = (place_of, side_links, corner_links)
    near = exchange(borders(tiles_in))
    hidden, bundle = conv(tiles_in, near, *links, first_bias, first, False)
    near = exchange(bundle)
    return conv(hidden, near, *links, second_bias, second, True)[0]


def solution(mesh):
    placed = (
        P(AXES, None, None, None),
        P("fsdp", None),
        P(),
        P("fsdp", None),
        P(),
        P(AXES, None, None),
        P(AXES, None, None),
    )
    return jax.shard_map(
        shards,
        mesh=mesh,
        in_specs=placed,
        out_specs=P(AXES, None, None, None),
        check_vma=False,
    )
```

```python
import functools

import jax
import jax.numpy as jnp
from jax import lax
from jax.experimental import pallas as pl
from jax.experimental.pallas import tpu as pltpu
from jax.sharding import PartitionSpec as P


AXES = ("tile", "fsdp")
PAD = 16


def move(x, target):
    rows, cols = (lax.axis_size("tile"), lax.axis_size("fsdp"))
    pairs = []
    for t in range(rows):
        for f in range(cols):
            there_t, there_f = target(t, f)
            pairs.append((t * cols + f, (there_t % rows) * cols + there_f % cols))
    return lax.ppermute(x, AXES, pairs)


def shift(x, rows, cols):
    return move(x, lambda t, f: (t + rows, f + cols))


def gather_rows(weight):
    rows, cols = (lax.axis_size("tile"), lax.axis_size("fsdp"))
    tall = rows // 4
    share = weight.shape[0] // rows
    width = weight.shape[1]
    parts = weight.reshape(rows, share, width)
    mine = lax.dynamic_index_in_dim(parts, lax.axis_index("tile"), 0, keepdims=True)
    unit = jnp.concatenate([shift(mine, 0, k) for k in range(1, cols)], axis=0)
    near = [unit]
    for step in range(1, 2 * tall):
        dy, dx = divmod(step, 2)
        near.append(
            move(
                unit, lambda t, f: (((t // 4 + dy) % tall) * 4 + ((t // 2 % 2) ^ dx) * 2 + t % 2, f)
            )
        )
    other = [move(x, lambda t, f: (t ^ 1, f)) for x in near]
    return near + other


def place(weight, pieces):
    rows, cols = (lax.axis_size("tile"), lax.axis_size("fsdp"))
    tall = rows // 4
    share, width = pieces[0].shape[1:]
    t, f = (lax.axis_index("tile"), lax.axis_index("fsdp"))
    pieces = jnp.concatenate(pieces, axis=0)
    source_f = jnp.arange(cols)[:, None]
    source_t = jnp.arange(rows)[None, :]
    core = (source_t ^ t) & 1
    dx = ((source_t ^ t) >> 1) & 1
    dy = (t // 4 - source_t // 4) % tall
    hop = (f - source_f) % cols
    index = (core * 2 * tall + dy * 2 + dx) * (cols - 1) + hop - 1
    index = jnp.where(hop == 0, 0, index)
    whole = jnp.take(pieces, index.reshape(-1), axis=0).reshape(cols, rows * share, width)
    whole = lax.dynamic_update_index_in_dim(whole, weight, f, 0)
    return whole.reshape(-1, width)


def gelu(x):
    return 0.5 * x * (1.0 + lax.erf(x * (0.5**0.5)))


def one_hot(rows, width, target):
    n = lax.broadcasted_iota(jnp.int32, (rows, width), 0)
    return jnp.where(lax.broadcasted_iota(jnp.int32, (rows, width), 1) == target(n), 1.0, 0.0).astype(
        jnp.bfloat16
    )


def select(picker, values):
    return jnp.dot(picker, values, preferred_element_type=jnp.float32)


def put_borders(bundle, tile, half, chunk, edge):
    rows = edge // 2
    sides = one_hot(
        edge, rows * edge, lambda n: jnp.where(n < rows, n * edge, (n - rows) * edge + edge - 1)
    )
    sides = select(sides, chunk).astype(jnp.bfloat16)
    start = tile * 4 * edge
    bundle[pl.ds(start + 3 * edge + half * rows, rows), :] = sides[:rows]
    bundle[pl.ds(start + edge + half * rows, rows), :] = sides[rows:]
    if half == 0:
        bundle[pl.ds(start, edge), :] = chunk[:edge]
    else:
        bundle[pl.ds(start + 2 * edge, edge), :] = chunk[-edge:]


def put_corners(bundle, tiles, edge):
    def source(n):
        corner = n & 3
        across = jnp.where((corner == 1) | (corner == 2), edge - 1, 0)
        return (n >> 2) * 4 * edge + jnp.where(corner >= 2, 2 * edge, 0) + across

    strips = tiles * 4 * edge
    cells = select(one_hot(PAD, strips, source), bundle[:strips, :])
    bundle[strips:, :] = cells.astype(jnp.bfloat16)


def borders_kernel(field, bundle):
    tiles, edge, _, channels = field.shape
    for tile in range(tiles):
        for half in range(2):
            rows = edge // 2
            chunk = field[tile, half * rows : (half + 1) * rows].reshape(rows * edge, channels)
            put_borders(bundle, tile, half, chunk, edge)
    put_corners(bundle, tiles, edge)


def borders(field):
    tiles, edge, _, channels = field.shape
    return pl.pallas_call(
        borders_kernel,
        out_shape=jax.ShapeDtypeStruct((tiles * 4 * edge + PAD, channels), jnp.bfloat16),
        name="borders",
    )(field)


def surround(field, near, side_links, corner_links, halos, wide):
    tiles, edge, _, channels = field.shape
    strips = tiles * 4 * edge
    column = lax.broadcasted_iota(jnp.int32, (edge, channels), 0)

    def put(tile, row, middle, before, after):
        spread = middle.astype(jnp.float32)
        left = jnp.where(column == 0, before, pltpu.roll(spread, 1, 0))
        right = jnp.where(column == edge - 1, after, pltpu.roll(spread, edge - 1, 0))
        wide[tile, row, :, :channels] = left.astype(jnp.bfloat16)
        wide[tile, row, :, channels : 2 * channels] = middle.astype(jnp.bfloat16)
        wide[tile, row, :, 2 * channels :] = right.astype(jnp.bfloat16)

    for tile in range(tiles):
        for side in range(4):
            link = (tile * 4 + side) * 3
            home = lax.rem(side_links[link], tiles) * 4 + side_links[link + 1]
            turns = (
                (1 if side >= 2 else 0)
                + jnp.where(side_links[link + 1] >= 2, 1, 0)
                + jnp.where(side_links[link + 2] == 1, 0, 1)
            )
            forward = lax.rem(turns, 2) == 0
            first = home * edge + jnp.where(forward, 0, edge - 1)
            step = jnp.where(forward, 1, -1)
            picker = one_hot(edge, strips, lambda n: first + step * n)
            halos[tile, side] = select(picker, near[side][:strips, :])
        cells = []
        for corner, (source, low) in enumerate(((3, 0), (1, 0), (1, PAD), (3, PAD))):
            link = (tile * 4 + corner) * 3
            pick = lax.rem(corner_links[link], tiles) * 4 + corner_links[link + 1]
            pick = jnp.where(corner_links[link + 2] == 1, pick, -1)
            picker = one_hot(8, PAD, lambda n: pick)
            cells.append(select(picker, near[source][strips + low : strips + low + PAD, :])[:1])
        put(tile, 0, halos[tile, 0], cells[0], cells[1])
        put(tile, edge + 1, halos[tile, 2], cells[3], cells[2])

        @pl.loop(0, edge // 4)
        def _(block):
            for offset in range(4):
                row = block * 4 + offset
                before = halos[tile, 3, pl.ds(row, 1), :]
                after = halos[tile, 1, pl.ds(row, 1), :]
                put(tile, row + 1, field[tile, row], before, after)


def fetch_weight(sources, whole, place_of, sems):
    copies = []
    if len(sources) == 1:
        copies.append(pltpu.make_async_copy(sources[0], whole, sems.at[0]))
    else:
        own, *pieces = sources
        hops, share, _ = pieces[0].shape
        steps = len(pieces) // 2
        cols = hops + 1
        rows = own.shape[0] // share
        t, f = (place_of[0], place_of[1])
        tall = steps // 2
        copies.append(
            pltpu.make_async_copy(
                own, whole.at[pl.ds(pl.multiple_of(f * rows * share, share), rows * share)], sems.at[0]
            )
        )
        for core in range(2):
            for step in range(steps):
                dy, dx = divmod(step, 2)
                far_y = lax.rem(t // 4 + tall - dy, tall)
                far_x = lax.rem(t // 2 + dx, 2)
                far = far_y * 4 + far_x * 2 + lax.rem(t + core, 2)
                for hop in range(1, cols):
                    far_f = lax.rem(f + cols - hop, cols)
                    start = pl.multiple_of((far_f * rows + far) * share, share)
                    copies.append(
                        pltpu.make_async_copy(
                            pieces[core * steps + step].at[hop - 1], whole.at[pl.ds(start, share)], sems.at[len(copies)]
                        )
                    )
    for copy in copies:
        copy.start()
    return copies


def conv_kernel(count, pooling, *refs):
    place_of, side_links, corner_links, field, north, east, south, west, bias = refs[:9]
    sources = refs[9 : 9 + count]
    outs = refs[9 + count : -5]
    halos, wide, whole, sems, total = refs[-5:]
    tiles, edge, _, channels = field.shape
    copies = fetch_weight(sources, whole, place_of, sems)
    surround(field, (north, east, south, west), side_links, corner_links, halos, wide)
    for copy in copies:
        copy.wait()
    rows = edge // 2
    depth = 3 * channels
    for tile in range(tiles):
        for half in range(2):
            low = half * rows
            summed = bias[...]
            for tap in range(3):
                window = wide[tile, low + tap : low + tap + rows].reshape(rows * edge, depth)
                summed = summed + lax.dot_general(
                    window,
                    whole[:, tap * depth : (tap + 1) * depth],
                    (((1,), (1,)), ((), ())),
                    preferred_element_type=jnp.float32,
                )
            act = gelu(summed)
            if pooling:
                width = act.shape[1]
                act = act.reshape(rows // 2, 2, edge, width)
                act = (act[:, 0] + act[:, 1]).reshape(rows // 2 * edge, width)
                mean = []
                for lanes in range(0, width, 128):
                    total[...] = act[:, lanes : lanes + 128]
                    even = total[pl.ds(0, rows * edge // 4, stride=2), :]
                    odd = total[pl.ds(1, rows * edge // 4, stride=2), :]
                    mean.append(((even + odd) * 0.25).astype(jnp.bfloat16))
                mean = jnp.concatenate(mean, axis=1)
                outs[0][tile, low // 2 : (low + rows) // 2] = mean.reshape(rows // 2, edge // 2, width)
            else:
                hidden = act.astype(jnp.bfloat16)
                outs[0][tile, low : low + rows] = hidden.reshape(rows, edge, act.shape[1])
                put_borders(outs[1], tile, half, hidden, edge)
    if not pooling:
        put_corners(outs[1], tiles, edge)


def conv(field, near, place_of, side_links, corner_links, bias, sources, pooling):
    tiles, edge, _, channels = field.shape
    width = bias.shape[0]
    if pooling:
        outs = (jax.ShapeDtypeStruct((tiles, edge // 2, edge // 2, width), jnp.bfloat16),)
    else:
        outs = (
            jax.ShapeDtypeStruct((tiles, edge, edge, width), jnp.bfloat16),
            jax.ShapeDtypeStruct((tiles * 4 * edge + PAD, width), jnp.bfloat16),
        )
    vmem = pl.BlockSpec(memory_space=pltpu.VMEM)
    smem = pl.BlockSpec(memory_space=pltpu.SMEM)
    anywhere = pl.BlockSpec(memory_space=pl.ANY)
    copies = 1 + sum(piece.shape[0] for piece in sources[1:])
    flops = 2 * tiles * edge * edge * 9 * channels * width
    return pl.pallas_call(
        functools.partial(conv_kernel, len(sources), pooling),
        out_shape=outs,
        in_specs=[smem] * 3 + [vmem] * 6 + [anywhere] * len(sources),
        out_specs=[vmem] * len(outs),
        scratch_shapes=[
            pltpu.VMEM((tiles, 4, edge, channels), jnp.float32),
            pltpu.VMEM((tiles, edge + 2, edge, 3 * channels), jnp.bfloat16),
            pltpu.VMEM((width, 9 * channels), jnp.bfloat16),
            pltpu.SemaphoreType.DMA((copies,)),
            pltpu.VMEM((edge * edge // 4, 128), jnp.float32),
        ],
        cost_estimate=pl.CostEstimate(flops=flops, bytes_accessed=8 << 20, transcendentals=0),
        name="second" if pooling else "first",
    )(
        place_of,
        side_links.reshape(-1),
        corner_links.reshape(-1),
        field,
        *near,
        bias.reshape(1, width),
        *sources,
    )


def exchange(bundle):
    north = shift(bundle, 1, 0)
    south = shift(bundle, -1, 0)
    strips = bundle.shape[0] - PAD
    bundle = jnp.concatenate([bundle[:strips], north[strips:], south[strips:]], axis=0)
    west = shift(bundle, 0, 1)
    east = shift(bundle, 0, -1)
    return north, east, south, west


def sources_of(weight):
    pieces = gather_rows(weight)
    if pieces[0].shape[1] % 16 == 0:
        return (weight, *pieces)
    return (place(weight, pieces),)


def shards(
    tiles_in, first_weight, first_bias, second_weight, second_bias, side_links, corner_links
):
    place_of = jnp.stack([lax.axis_index("tile"), lax.axis_index("fsdp")])
    first = sources_of(first_weight)
    second = sources_of(second_weight)
    links = (place_of, side_links, corner_links)
    bundle = borders(tiles_in)
    near = exchange(bundle)
    hidden, bundle = conv(tiles_in, near, *links, first_bias, first, False)
    near = exchange(bundle)
    return conv(hidden, near, *links, second_bias, second, True)[0]


def solution(mesh):
    placed = (
        P(AXES, None, None, None),
        P("fsdp", None),
        P(),
        P("fsdp", None),
        P(),
        P(AXES, None, None),
        P(AXES, None, None),
    )
    return jax.shard_map(
        shards,
        mesh=mesh,
        in_specs=placed,
        out_specs=P(AXES, None, None, None),
        check_vma=False,
    )
```

```python
import functools

import jax
import jax.numpy as jnp
from jax import lax
from jax.experimental import pallas as pl
from jax.experimental.pallas import tpu as pltpu
from jax.sharding import PartitionSpec as P


AXES = ("tile", "fsdp")
PAD = 16
GRANT = 36 << 20


def move(x, target):
    rows, cols = (lax.axis_size("tile"), lax.axis_size("fsdp"))
    pairs = []
    for t in range(rows):
        for f in range(cols):
            there_t, there_f = target(t, f)
            pairs.append((t * cols + f, (there_t % rows) * cols + there_f % cols))
    return lax.ppermute(x, AXES, pairs)


def shift(x, rows, cols):
    return move(x, lambda t, f: (t + rows, f + cols))


def doublings(cols):
    bits = [1 << k for k in range(cols.bit_length() - 1)]
    return bits[::-1]


def gather_rows(weight):
    rows, cols = (lax.axis_size("tile"), lax.axis_size("fsdp"))
    tall = rows // 4
    share = weight.shape[0] // rows
    width = weight.shape[1]
    parts = weight.reshape(rows, share, width)
    mine = lax.dynamic_index_in_dim(parts, lax.axis_index("tile"), 0, keepdims=True)
    held = {0: mine}
    for bit in doublings(cols):
        there = jnp.concatenate([held[h] for h in sorted(held)], axis=0)
        there = move(there, lambda t, f: (t, f ^ bit))
        held.update({h ^ bit: there[i : i + 1] for i, h in enumerate(sorted(held))})
    unit = jnp.concatenate([held[h] for h in range(1, cols)], axis=0)
    near = [unit]
    for step in range(1, 2 * tall):
        dy, dx = divmod(step, 2)
        near.append(move(unit, lambda t, f: (((t // 4 + dy) % tall) * 4 + ((t // 2 % 2) ^ dx) * 2 + t % 2, f)))
    other = [move(x, lambda t, f: (t ^ 1, f)) for x in near]
    return near + other


def place(weight, pieces):
    rows, cols = (lax.axis_size("tile"), lax.axis_size("fsdp"))
    tall = rows // 4
    share, width = pieces[0].shape[1:]
    t, f = (lax.axis_index("tile"), lax.axis_index("fsdp"))
    pieces = jnp.concatenate(pieces, axis=0)
    source_f = jnp.arange(cols)[:, None]
    source_t = jnp.arange(rows)[None, :]
    core = (source_t ^ t) & 1
    dx = ((source_t ^ t) >> 1) & 1
    dy = (t // 4 - source_t // 4) % tall
    hop = f ^ source_f
    index = (core * 2 * tall + dy * 2 + dx) * (cols - 1) + hop - 1
    index = jnp.where(hop == 0, 0, index)
    whole = jnp.take(pieces, index.reshape(-1), axis=0).reshape(cols, rows * share, width)
    whole = lax.dynamic_update_index_in_dim(whole, weight, f, 0)
    return whole.reshape(-1, width)


def gelu(x):
    return 0.5 * x * (1.0 + lax.erf(x * (0.5**0.5)))


def one_hot(rows, width, target):
    n = lax.broadcasted_iota(jnp.int32, (rows, width), 0)
    return jnp.where(lax.broadcasted_iota(jnp.int32, (rows, width), 1) == target(n), 1.0, 0.0).astype(
        jnp.bfloat16
    )


def select(picker, values):
    return jnp.dot(picker, values, preferred_element_type=jnp.float32)


def put_borders(bundle, tile, half, chunk, edge):
    rows = edge // 2
    sides = one_hot(
        edge, rows * edge, lambda n: jnp.where(n < rows, n * edge, (n - rows) * edge + edge - 1)
    )
    sides = select(sides, chunk).astype(jnp.bfloat16)
    start = tile * 4 * edge
    bundle[pl.ds(start + 3 * edge + half * rows, rows), :] = sides[:rows]
    bundle[pl.ds(start + edge + half * rows, rows), :] = sides[rows:]
    if half == 0:
        bundle[pl.ds(start, edge), :] = chunk[:edge]
    else:
        bundle[pl.ds(start + 2 * edge, edge), :] = chunk[-edge:]


def request_of(links, link, tiles, edge, turned):
    home = lax.rem(links[link], tiles) * 4 + links[link + 1]
    turns = turned + jnp.where(links[link + 1] >= 2, 1, 0) + jnp.where(links[link + 2] == 1, 0, 1)
    forward = lax.rem(turns, 2) == 0
    return home * edge + jnp.where(forward, 0, edge - 1), jnp.where(forward, 1, -1)


def put_corners(bundle, tiles, edge, links=None):
    def source(n):
        corner = n & 3
        across = jnp.where((corner == 1) | (corner == 2), edge - 1, 0)
        return (n >> 2) * 4 * edge + jnp.where(corner >= 2, 2 * edge, 0) + across

    strips = tiles * 4 * edge
    cells = select(one_hot(PAD, strips, source), bundle[:strips, :])
    if links is not None:
        row = lax.broadcasted_iota(jnp.int32, cells.shape, 0)
        lane = lax.broadcasted_iota(jnp.int32, cells.shape, 1)
        for side in range(tiles * 4):
            first, step = request_of(links, 2 + side * 3, tiles, edge, 1 if side % 4 >= 2 else 0)
            asked = jnp.where(lane < 128, first, step).astype(jnp.float32)
            cells = jnp.where(row == tiles * 4 + side, asked, cells)
    bundle[strips:, :] = cells.astype(jnp.bfloat16)


def answer(out, bundle, near, side, tiles, edge):
    strips = tiles * 4 * edge
    asked = near[strips : strips + PAD, :256].astype(jnp.float32)
    n = lax.broadcasted_iota(jnp.int32, (edge, strips), 0).astype(jnp.float32)
    column = lax.broadcasted_iota(jnp.int32, (edge, strips), 1).astype(jnp.float32)
    for tile in range(tiles):
        row = tiles * 4 + tile * 4 + side
        first, step = (
            jnp.concatenate([asked[row : row + 1, low : low + 128]] * (strips // 128), axis=1)
            for low in (0, 128)
        )
        picker = jnp.where(column == first + step * n, 1.0, 0.0).astype(jnp.bfloat16)
        out[tile * edge : (tile + 1) * edge, :] = select(picker, bundle[:strips, :]).astype(jnp.bfloat16)


def borders_kernel(links, field, bundle):
    tiles, edge, _, channels = field.shape
    for tile in range(tiles):
        for half in range(2):
            rows = edge // 2
            chunk = field[tile, half * rows : (half + 1) * rows].reshape(rows * edge, channels)
            put_borders(bundle, tile, half, chunk, edge)
    put_corners(bundle, tiles, edge, links)


def borders(field, links):
    tiles, edge, _, channels = field.shape
    return pl.pallas_call(
        borders_kernel,
        out_shape=jax.ShapeDtypeStruct((tiles * 4 * edge + PAD, channels), jnp.bfloat16),
        in_specs=[pl.BlockSpec(memory_space=pltpu.SMEM), pl.BlockSpec(memory_space=pltpu.VMEM)],
        out_specs=pl.BlockSpec(memory_space=pltpu.VMEM),
        compiler_params=pltpu.CompilerParams(vmem_limit_bytes=16 << 20),
        name="borders",
    )(links, field)


def surround(field, near, links, chosen, halos, wide):
    tiles, edge, _, channels = field.shape
    strips = tiles * edge if chosen else tiles * 4 * edge
    cells_at = strips if chosen else strips + PAD
    column = lax.broadcasted_iota(jnp.int32, (edge, channels), 0)

    def put(tile, row, middle, before, after):
        spread = middle.astype(jnp.float32)
        left = jnp.where(column == 0, before, pltpu.roll(spread, 1, 0))
        right = jnp.where(column == edge - 1, after, pltpu.roll(spread, edge - 1, 0))
        wide[tile, row, :, :channels] = left.astype(jnp.bfloat16)
        wide[tile, row, :, channels : 2 * channels] = middle.astype(jnp.bfloat16)
        wide[tile, row, :, 2 * channels :] = right.astype(jnp.bfloat16)

    for tile in range(tiles):
        for side in range(4):
            if chosen:
                halos[tile, side] = near[side][tile * edge : (tile + 1) * edge, :].astype(jnp.float32)
                continue
            first, step = request_of(
                links, 2 + (tile * 4 + side) * 3, tiles, edge, 1 if side >= 2 else 0
            )
            picker = one_hot(edge, strips, lambda n: first + step * n)
            halos[tile, side] = select(picker, near[side][:strips, :])
        cells = []
        for corner, (source, low) in enumerate(((3, 0), (1, 0), (1, PAD), (3, PAD))):
            link = 2 + (tiles * 4 + tile * 4 + corner) * 3
            pick = lax.rem(links[link], tiles) * 4 + links[link + 1]
            pick = jnp.where(links[link + 2] == 1, pick, -1)
            picker = one_hot(8, PAD, lambda n: pick)
            cells.append(select(picker, near[source][cells_at + low : cells_at + low + PAD, :])[:1])
        put(tile, 0, halos[tile, 0], cells[0], cells[1])
        put(tile, edge + 1, halos[tile, 2], cells[3], cells[2])

        @pl.loop(0, edge // 4)
        def _(block):
            for offset in range(4):
                row = block * 4 + offset
                before = halos[tile, 3, pl.ds(row, 1), :]
                after = halos[tile, 1, pl.ds(row, 1), :]
                put(tile, row + 1, field[tile, row], before, after)


def fetch_weight(sources, whole, links, sems):
    copies = []
    if len(sources) == 1:
        copies.append(pltpu.make_async_copy(sources[0], whole, sems.at[0]))
    else:
        own, *pieces = sources
        hops, share, _ = pieces[0].shape
        steps = len(pieces) // 2
        cols = hops + 1
        rows = own.shape[0] // share
        t, f = (links[0], links[1])
        tall = steps // 2
        copies.append(
            pltpu.make_async_copy(
                own, whole.at[pl.ds(pl.multiple_of(f * rows * share, share), rows * share)], sems.at[0]
            )
        )
        for core in range(2):
            for step in range(steps):
                dy, dx = divmod(step, 2)
                far_y = lax.rem(t // 4 + tall - dy, tall)
                far_x = lax.rem(t // 2 + dx, 2)
                far = far_y * 4 + far_x * 2 + lax.rem(t + core, 2)
                for hop in range(1, cols):
                    far_f = f ^ hop
                    start = pl.multiple_of((far_f * rows + far) * share, share)
                    copies.append(
                        pltpu.make_async_copy(
                            pieces[core * steps + step].at[hop - 1], whole.at[pl.ds(start, share)], sems.at[len(copies)]
                        )
                    )
    for copy in copies:
        copy.start()
    return copies


def conv_kernel(count, pooling, *refs):
    links, field, north, east, south, west, bias = refs[:7]
    near = (north, east, south, west)
    sources = refs[7 : 7 + count]
    outs = refs[7 + count : -6]
    halos, wide, whole, sems, total, bundle = refs[-6:]
    tiles, edge, _, channels = field.shape
    copies = fetch_weight(sources, whole, links, sems)
    surround(field, near, links, pooling, halos, wide)
    for copy in copies:
        copy.wait()
    rows = edge // 2
    depth = 3 * channels
    for tile in range(tiles):
        for half in range(2):
            low = half * rows
            summed = bias[...]
            for tap in range(3):
                window = wide[tile, low + tap : low + tap + rows].reshape(rows * edge, depth)
                summed = summed + lax.dot_general(
                    window,
                    whole[:, tap * depth : (tap + 1) * depth],
                    (((1,), (1,)), ((), ())),
                    preferred_element_type=jnp.float32,
                )
            act = gelu(summed)
            if pooling:
                width = act.shape[1]
                act = act.reshape(rows // 2, 2, edge, width)
                act = (act[:, 0] + act[:, 1]).reshape(rows // 2 * edge, width)
                mean = []
                for lanes in range(0, width, 128):
                    total[...] = act[:, lanes : lanes + 128]
                    even = total[pl.ds(0, rows * edge // 4, stride=2), :]
                    odd = total[pl.ds(1, rows * edge // 4, stride=2), :]
                    mean.append(((even + odd) * 0.25).astype(jnp.bfloat16))
                mean = jnp.concatenate(mean, axis=1)
                outs[0][tile, low // 2 : (low + rows) // 2] = mean.reshape(rows // 2, edge // 2, width)
            else:
                hidden = act.astype(jnp.bfloat16)
                outs[0][tile, low : low + rows] = hidden.reshape(rows, edge, act.shape[1])
                put_borders(bundle, tile, half, hidden, edge)
    if not pooling:
        put_corners(bundle, tiles, edge)
        for side, out in enumerate(outs[1:]):
            answer(out, bundle, near[side], (side + 2) % 4, tiles, edge)
            if side in (0, 2):
                out[tiles * edge :, :] = bundle[tiles * 4 * edge :, :]


def conv(field, near, links, bias, sources, pooling):
    tiles, edge, _, channels = field.shape
    width = bias.shape[0]
    if pooling:
        outs = (jax.ShapeDtypeStruct((tiles, edge // 2, edge // 2, width), jnp.bfloat16),)
    else:
        outs = (jax.ShapeDtypeStruct((tiles, edge, edge, width), jnp.bfloat16),) + tuple(
            jax.ShapeDtypeStruct((tiles * edge + extra, width), jnp.bfloat16) for extra in (PAD, 0, PAD, 0)
        )
    vmem = pl.BlockSpec(memory_space=pltpu.VMEM)
    smem = pl.BlockSpec(memory_space=pltpu.SMEM)
    anywhere = pl.BlockSpec(memory_space=pl.ANY)
    copies = 1 + sum(piece.shape[0] for piece in sources[1:])
    flops = 2 * tiles * edge * edge * 9 * channels * width
    return pl.pallas_call(
        functools.partial(conv_kernel, len(sources), pooling),
        out_shape=outs,
        in_specs=[smem] + [vmem] * 6 + [anywhere] * len(sources),
        out_specs=[vmem] * len(outs),
        scratch_shapes=[
            pltpu.VMEM((tiles, 4, edge, channels), jnp.float32),
            pltpu.VMEM((tiles, edge + 2, edge, 3 * channels), jnp.bfloat16),
            pltpu.VMEM((width, 9 * channels), jnp.bfloat16),
            pltpu.SemaphoreType.DMA((copies,)),
            pltpu.VMEM((edge * edge // 4, 128), jnp.float32),
            pltpu.VMEM((tiles * 4 * edge + PAD, width), jnp.bfloat16),
        ],
        cost_estimate=pl.CostEstimate(flops=flops, bytes_accessed=8 << 20, transcendentals=0),
        compiler_params=pltpu.CompilerParams(vmem_limit_bytes=GRANT),
        name="second" if pooling else "first",
    )(
        links,
        field,
        *near,
        bias.reshape(1, width),
        *sources,
    )


def exchange(to_north, to_east, to_south, to_west):
    north = shift(to_south, 1, 0)
    south = shift(to_north, -1, 0)
    cells = [north[-PAD:], south[-PAD:]]
    west = shift(jnp.concatenate([to_east, *cells], axis=0), 0, 1)
    east = shift(jnp.concatenate([to_west, *cells], axis=0), 0, -1)
    return north, east, south, west


def sources_of(weight):
    pieces = gather_rows(weight)
    if pieces[0].shape[1] % 16 == 0:
        return (weight, *pieces)
    return (place(weight, pieces),)


def shards(
    tiles_in, first_weight, first_bias, second_weight, second_bias, side_links, corner_links
):
    links = jnp.concatenate(
        [
            lax.axis_index("tile").reshape(1),
            lax.axis_index("fsdp").reshape(1),
            side_links.reshape(-1),
            corner_links.reshape(-1),
        ]
    )
    first = sources_of(first_weight)
    second = sources_of(second_weight)
    bundle = borders(tiles_in, links)
    near = exchange(bundle, bundle, bundle, bundle)
    hidden, *strips = conv(tiles_in, near, links, first_bias, first, False)
    near = exchange(*strips)
    return conv(hidden, near, links, second_bias, second, True)[0]


def solution(mesh):
    placed = (
        P(AXES, None, None, None),
        P("fsdp", None),
        P(),
        P("fsdp", None),
        P(),
        P(AXES, None, None),
        P(AXES, None, None),
    )
    return jax.shard_map(
        shards,
        mesh=mesh,
        in_specs=placed,
        out_specs=P(AXES, None, None, None),
        check_vma=False,
    )
```

```python
import functools

import jax
import jax.numpy as jnp
from jax import lax
from jax.experimental import pallas as pl
from jax.experimental.pallas import tpu as pltpu
from jax.sharding import PartitionSpec as P


AXES = ("tile", "fsdp")
PAD = 16
GRANT = 36 << 20


def move(x, target):
    rows, cols = (lax.axis_size("tile"), lax.axis_size("fsdp"))
    pairs = []
    for t in range(rows):
        for f in range(cols):
            there_t, there_f = target(t, f)
            pairs.append((t * cols + f, (there_t % rows) * cols + there_f % cols))
    return lax.ppermute(x, AXES, pairs)


def shift(x, rows, cols):
    return move(x, lambda t, f: (t + rows, f + cols))


def doublings(cols):
    bits = [1 << k for k in range(cols.bit_length() - 1)]
    return bits[::-1]


def across(x, dy, dx):
    tall = lax.axis_size("tile") // 4
    return move(x, lambda t, f: (((t // 4 + dy) % tall) * 4 + ((t // 2 % 2) ^ dx) * 2 + t % 2, f))


def gather_rows(weight, relay):
    rows, cols = (lax.axis_size("tile"), lax.axis_size("fsdp"))
    tall = rows // 4
    share = weight.shape[0] // rows
    width = weight.shape[1]
    parts = weight.reshape(rows, share, width)
    mine = lax.dynamic_index_in_dim(parts, lax.axis_index("tile"), 0, keepdims=True)
    held = {0: mine}
    for bit in doublings(cols):
        there = jnp.concatenate([held[h] for h in sorted(held)], axis=0)
        there = move(there, lambda t, f: (t, f ^ bit))
        held.update({h ^ bit: there[i : i + 1] for i, h in enumerate(sorted(held))})
    unit = jnp.concatenate([held[h] for h in range(1, cols)], axis=0)
    sent = [(unit, 0, 0)]
    for step in range(1, 2 * tall):
        if not (relay and step == 3):
            sent.append((across(unit, *divmod(step, 2)), step, 0))
    if relay:
        half = width // 2
        by_x, by_y = (sent[1][0], sent[2][0])
        sent.append((across(by_x[:, :, :half], 1, 0), 3, 0))
        sent.append((across(by_y[:, :, half:], 0, 1), 3, half))
    other = [move(x, lambda t, f: (t ^ 1, f)) for x, _, _ in sent]
    places = [(0, *place[1:]) for place in sent] + [(1, *place[1:]) for place in sent]
    return [x for x, _, _ in sent] + other, places


def place(weight, pieces):
    rows, cols = (lax.axis_size("tile"), lax.axis_size("fsdp"))
    tall = rows // 4
    share, width = pieces[0].shape[1:]
    t, f = (lax.axis_index("tile"), lax.axis_index("fsdp"))
    pieces = jnp.concatenate(pieces, axis=0)
    source_f = jnp.arange(cols)[:, None]
    source_t = jnp.arange(rows)[None, :]
    core = (source_t ^ t) & 1
    dx = ((source_t ^ t) >> 1) & 1
    dy = (t // 4 - source_t // 4) % tall
    hop = f ^ source_f
    index = (core * 2 * tall + dy * 2 + dx) * (cols - 1) + hop - 1
    index = jnp.where(hop == 0, 0, index)
    whole = jnp.take(pieces, index.reshape(-1), axis=0).reshape(cols, rows * share, width)
    whole = lax.dynamic_update_index_in_dim(whole, weight, f, 0)
    return whole.reshape(-1, width)


def gelu(x):
    return 0.5 * x * (1.0 + lax.erf(x * (0.5**0.5)))


def one_hot(rows, width, target):
    n = lax.broadcasted_iota(jnp.int32, (rows, width), 0)
    return jnp.where(lax.broadcasted_iota(jnp.int32, (rows, width), 1) == target(n), 1.0, 0.0).astype(
        jnp.bfloat16
    )


def select(picker, values):
    return jnp.dot(picker, values, preferred_element_type=jnp.float32)


def put_borders(bundle, tile, half, chunk, edge):
    rows = edge // 2
    sides = one_hot(
        edge, rows * edge, lambda n: jnp.where(n < rows, n * edge, (n - rows) * edge + edge - 1)
    )
    sides = select(sides, chunk).astype(jnp.bfloat16)
    start = tile * 4 * edge
    bundle[pl.ds(start + 3 * edge + half * rows, rows), :] = sides[:rows]
    bundle[pl.ds(start + edge + half * rows, rows), :] = sides[rows:]
    if half == 0:
        bundle[pl.ds(start, edge), :] = chunk[:edge]
    else:
        bundle[pl.ds(start + 2 * edge, edge), :] = chunk[-edge:]


def request_of(links, tile, side, tiles, edge):
    near_id, near_side, flag = (links[i, tile, side] for i in range(3))
    home = lax.rem(near_id, tiles) * 4 + near_side
    turns = (1 if side >= 2 else 0) + jnp.where(near_side >= 2, 1, 0) + jnp.where(flag == 1, 0, 1)
    forward = lax.rem(turns, 2) == 0
    return home * edge + jnp.where(forward, 0, edge - 1), jnp.where(forward, 1, -1)


def put_corners(bundle, tiles, edge, links=None):
    def source(n):
        corner = n & 3
        across = jnp.where((corner == 1) | (corner == 2), edge - 1, 0)
        return (n >> 2) * 4 * edge + jnp.where(corner >= 2, 2 * edge, 0) + across

    strips = tiles * 4 * edge
    cells = select(one_hot(PAD, strips, source), bundle[:strips, :])
    if links is not None:
        row = lax.broadcasted_iota(jnp.int32, cells.shape, 0)
        lane = lax.broadcasted_iota(jnp.int32, cells.shape, 1)
        for side in range(tiles * 4):
            first, step = request_of(links, side // 4, side % 4, tiles, edge)
            asked = jnp.where(lane < 128, first, step).astype(jnp.float32)
            cells = jnp.where(row == tiles * 4 + side, asked, cells)
    bundle[strips:, :] = cells.astype(jnp.bfloat16)


def answer(out, bundle, near, side, tiles, edge):
    strips = tiles * 4 * edge
    asked = near[strips : strips + PAD, :256].astype(jnp.float32)
    n = lax.broadcasted_iota(jnp.int32, (edge, strips), 0).astype(jnp.float32)
    column = lax.broadcasted_iota(jnp.int32, (edge, strips), 1).astype(jnp.float32)
    for tile in range(tiles):
        row = tiles * 4 + tile * 4 + side
        first, step = (
            jnp.concatenate([asked[row : row + 1, low : low + 128]] * (strips // 128), axis=1)
            for low in (0, 128)
        )
        picker = jnp.where(column == first + step * n, 1.0, 0.0).astype(jnp.bfloat16)
        out[tile * edge : (tile + 1) * edge, :] = select(picker, bundle[:strips, :]).astype(jnp.bfloat16)


def borders_kernel(links, field, bundle):
    tiles, edge, _, channels = field.shape
    for tile in range(tiles):
        for half in range(2):
            rows = edge // 2
            chunk = field[tile, half * rows : (half + 1) * rows].reshape(rows * edge, channels)
            put_borders(bundle, tile, half, chunk, edge)
    put_corners(bundle, tiles, edge, links)


def borders(field, links):
    tiles, edge, _, channels = field.shape
    return pl.pallas_call(
        borders_kernel,
        out_shape=jax.ShapeDtypeStruct((tiles * 4 * edge + PAD, channels), jnp.bfloat16),
        in_specs=[pl.BlockSpec(memory_space=pltpu.SMEM), pl.BlockSpec(memory_space=pltpu.VMEM)],
        out_specs=pl.BlockSpec(memory_space=pltpu.VMEM),
        compiler_params=pltpu.CompilerParams(vmem_limit_bytes=16 << 20),
        name="borders",
    )(links, field)


def surround(field, near, side_links, corner_links, chosen, halos, wide):
    tiles, edge, _, channels = field.shape
    strips = tiles * edge if chosen else tiles * 4 * edge
    cells_at = strips if chosen else strips + PAD
    column = lax.broadcasted_iota(jnp.int32, (edge, channels), 0)

    def put(tile, row, middle, before, after):
        spread = middle.astype(jnp.float32)
        left = jnp.where(column == 0, before, pltpu.roll(spread, 1, 0))
        right = jnp.where(column == edge - 1, after, pltpu.roll(spread, edge - 1, 0))
        wide[tile, row, :, :channels] = left.astype(jnp.bfloat16)
        wide[tile, row, :, channels : 2 * channels] = middle.astype(jnp.bfloat16)
        wide[tile, row, :, 2 * channels :] = right.astype(jnp.bfloat16)

    for tile in range(tiles):
        for side in range(4):
            if chosen:
                halos[tile, side] = near[side][tile * edge : (tile + 1) * edge, :].astype(jnp.float32)
                continue
            first, step = request_of(side_links, tile, side, tiles, edge)
            picker = one_hot(edge, strips, lambda n: first + step * n)
            halos[tile, side] = select(picker, near[side][:strips, :])
        cells = []
        for corner, (source, low) in enumerate(((3, 0), (1, 0), (1, PAD), (3, PAD))):
            near_id, near_corner, flag = (corner_links[i, tile, corner] for i in range(3))
            pick = jnp.where(flag == 1, lax.rem(near_id, tiles) * 4 + near_corner, -1)
            picker = one_hot(8, PAD, lambda n: pick)
            cells.append(select(picker, near[source][cells_at + low : cells_at + low + PAD, :])[:1])
        put(tile, 0, halos[tile, 0], cells[0], cells[1])
        put(tile, edge + 1, halos[tile, 2], cells[3], cells[2])

        @pl.loop(0, edge // 4)
        def _(block):
            for offset in range(4):
                row = block * 4 + offset
                before = halos[tile, 3, pl.ds(row, 1), :]
                after = halos[tile, 1, pl.ds(row, 1), :]
                put(tile, row + 1, field[tile, row], before, after)


def fetch_weight(sources, places, whole, place_of):
    own, *pieces = sources
    hops, share, _ = pieces[0].shape
    rows = own.shape[0] // share
    t, f = (place_of[0], place_of[1])
    tall = rows // 4
    whole[pl.ds(pl.multiple_of(f * rows * share, share), rows * share), :] = own[...]
    for piece, (core, step, low) in zip(pieces, places):
        dy, dx = divmod(step, 2)
        far_y = lax.rem(t // 4 + tall - dy, tall)
        far_x = lax.rem(t // 2 + dx, 2)
        far = far_y * 4 + far_x * 2 + lax.rem(t + core, 2)
        for hop in range(1, hops + 1):
            start = pl.multiple_of(((f ^ hop) * rows + far) * share, share)
            whole[pl.ds(start, share), low : low + piece.shape[2]] = piece[hop - 1]


def conv_kernel(places, pooling, *refs):
    place_of, side_links, corner_links, field, north, east, south, west, bias = refs[:9]
    near = (north, east, south, west)
    count = 1 + len(places)
    sources = refs[9 : 9 + count]
    outs = refs[9 + count : -5]
    halos, wide, whole, total, bundle = refs[-5:]
    tiles, edge, _, channels = field.shape
    if count == 1:
        whole = sources[0]
    else:
        fetch_weight(sources, places, whole, place_of)
    surround(field, near, side_links, corner_links, pooling, halos, wide)
    rows = edge // 2
    depth = 3 * channels
    for tile in range(tiles):
        for half in range(2):
            low = half * rows
            summed = bias[...]
            for tap in range(3):
                window = wide[tile, low + tap : low + tap + rows].reshape(rows * edge, depth)
                summed = summed + lax.dot_general(
                    window,
                    whole[:, tap * depth : (tap + 1) * depth],
                    (((1,), (1,)), ((), ())),
                    preferred_element_type=jnp.float32,
                )
            act = gelu(summed)
            if pooling:
                width = act.shape[1]
                act = act.reshape(rows // 2, 2, edge, width)
                act = (act[:, 0] + act[:, 1]).reshape(rows // 2 * edge, width)
                mean = []
                for lanes in range(0, width, 128):
                    total[...] = act[:, lanes : lanes + 128]
                    even = total[pl.ds(0, rows * edge // 4, stride=2), :]
                    odd = total[pl.ds(1, rows * edge // 4, stride=2), :]
                    mean.append(((even + odd) * 0.25).astype(jnp.bfloat16))
                mean = jnp.concatenate(mean, axis=1)
                outs[0][tile, low // 2 : (low + rows) // 2] = mean.reshape(rows // 2, edge // 2, width)
            else:
                hidden = act.astype(jnp.bfloat16)
                outs[0][tile, low : low + rows] = hidden.reshape(rows, edge, act.shape[1])
                put_borders(bundle, tile, half, hidden, edge)
    if not pooling:
        put_corners(bundle, tiles, edge)
        for side, out in enumerate(outs[1:]):
            answer(out, bundle, near[side], (side + 2) % 4, tiles, edge)
            if side in (0, 2):
                out[tiles * edge :, :] = bundle[tiles * 4 * edge :, :]


def conv(field, near, links, bias, weight, pooling):
    sources, places = weight
    tiles, edge, _, channels = field.shape
    width = bias.shape[0]
    if pooling:
        outs = (jax.ShapeDtypeStruct((tiles, edge // 2, edge // 2, width), jnp.bfloat16),)
    else:
        outs = (jax.ShapeDtypeStruct((tiles, edge, edge, width), jnp.bfloat16),) + tuple(
            jax.ShapeDtypeStruct((tiles * edge + extra, width), jnp.bfloat16) for extra in (PAD, 0, PAD, 0)
        )
    vmem = pl.BlockSpec(memory_space=pltpu.VMEM)
    smem = pl.BlockSpec(memory_space=pltpu.SMEM)
    flops = 2 * tiles * edge * edge * 9 * channels * width
    return pl.pallas_call(
        functools.partial(conv_kernel, places, pooling),
        out_shape=outs,
        in_specs=[smem] * 3 + [vmem] * (6 + len(sources)),
        out_specs=[vmem] * len(outs),
        scratch_shapes=[
            pltpu.VMEM((tiles, 4, edge, channels), jnp.float32),
            pltpu.VMEM((tiles, edge + 2, edge, 3 * channels), jnp.bfloat16),
            pltpu.VMEM((width if len(sources) > 1 else 8, 9 * channels), jnp.bfloat16),
            pltpu.VMEM((edge * edge // 4, 128), jnp.float32),
            pltpu.VMEM((tiles * 4 * edge + PAD, width), jnp.bfloat16),
        ],
        cost_estimate=pl.CostEstimate(flops=flops, bytes_accessed=8 << 20, transcendentals=0),
        compiler_params=pltpu.CompilerParams(vmem_limit_bytes=GRANT),
        name="second" if pooling else "first",
    )(
        *links,
        field,
        *near,
        bias.reshape(1, width),
        *sources,
    )


def exchange(to_north, to_east, to_south, to_west):
    north = shift(to_south, 1, 0)
    south = shift(to_north, -1, 0)
    cells = [north[-PAD:], south[-PAD:]]
    west = shift(jnp.concatenate([to_east, *cells], axis=0), 0, 1)
    east = shift(jnp.concatenate([to_west, *cells], axis=0), 0, -1)
    return north, east, south, west


def sources_of(weight, relay):
    pieces, places = gather_rows(weight, relay)
    if pieces[0].shape[1] % 16 == 0:
        return (weight, *pieces), tuple(places)
    return (place(weight, pieces),), ()


def shards(
    tiles_in, first_weight, first_bias, second_weight, second_bias, side_links, corner_links
):
    place_of = jnp.stack([lax.axis_index("tile"), lax.axis_index("fsdp")])
    side_links = side_links.transpose(2, 0, 1)
    links = (place_of, side_links, corner_links.transpose(2, 0, 1))
    first = sources_of(first_weight, False)
    second = sources_of(second_weight, lax.axis_size("tile") == 8)
    bundle = borders(tiles_in, side_links)
    near = exchange(bundle, bundle, bundle, bundle)
    hidden, *strips = conv(tiles_in, near, links, first_bias, first, False)
    near = exchange(*strips)
    return conv(hidden, near, links, second_bias, second, True)[0]


def solution(mesh):
    placed = (
        P(AXES, None, None, None),
        P("fsdp", None),
        P(),
        P("fsdp", None),
        P(),
        P(AXES, None, None),
        P(AXES, None, None),
    )
    return jax.shard_map(
        shards,
        mesh=mesh,
        in_specs=placed,
        out_specs=P(AXES, None, None, None),
        check_vma=False,
    )
```

```python
import functools

import jax
import jax.numpy as jnp
from jax import lax
from jax.experimental import pallas as pl
from jax.experimental.pallas import tpu as pltpu
from jax.sharding import PartitionSpec as P


AXES = ("tile", "fsdp")
PAD = 16
GRANT = 36 << 20


def move(x, target):
    rows, cols = (lax.axis_size("tile"), lax.axis_size("fsdp"))
    pairs = []
    for t in range(rows):
        for f in range(cols):
            there_t, there_f = target(t, f)
            pairs.append((t * cols + f, (there_t % rows) * cols + there_f % cols))
    return lax.ppermute(x, AXES, pairs)


def shift(x, rows, cols):
    return move(x, lambda t, f: (t + rows, f + cols))


def doublings(cols):
    bits = [1 << k for k in range(cols.bit_length() - 1)]
    return bits[::-1]


def across(x, dy, dx):
    tall = lax.axis_size("tile") // 4
    return move(x, lambda t, f: (((t // 4 + dy) % tall) * 4 + ((t // 2 % 2) ^ dx) * 2 + t % 2, f))


def gather_rows(weight, relay, asked):
    rows, cols = (lax.axis_size("tile"), lax.axis_size("fsdp"))
    tall = rows // 4
    share = weight.shape[0] // rows
    width = weight.shape[1]
    parts = weight.reshape(rows, share, width)
    mine = lax.dynamic_index_in_dim(parts, lax.axis_index("tile"), 0, keepdims=True)
    notes = None
    if asked is not None:
        mine = jnp.concatenate([mine, asked[None]], axis=2)
        parts = [shift(mine, 0, k) for k in range(1, cols)]
        hops = [(-k, 0) for k in range(1, cols)]
        notes = (parts[0], parts[-1])
    else:
        parts, hops = ([mine], [(0, 0)])
        for bit in doublings(cols):
            there = parts[0] if len(parts) == 1 else jnp.concatenate(parts, axis=0)
            parts.append(move(there, lambda t, f: (t, f ^ bit)))
            hops += [(0, hop ^ bit) for _, hop in hops]
        parts, hops = (parts[1:], hops[1:])
    unit = jnp.concatenate(parts, axis=0)
    sent = [(unit, 0, 0)]
    for step in range(1, 2 * tall):
        if not (relay and step == 3):
            sent.append((across(unit, *divmod(step, 2)), step, 0))
    if relay:
        half = width // 2
        by_x, by_y = (sent[1][0], sent[2][0])
        sent.append((across(by_x[:, :, :half], 1, 0), 3, 0))
        sent.append((across(by_y[:, :, half:], 0, 1), 3, half))
    other = [move(x, lambda t, f: (t ^ 1, f)) for x, _, _ in sent]
    places = [(0, *place[1:]) for place in sent] + [(1, *place[1:]) for place in sent]
    return [x for x, _, _ in sent] + other, places, hops, notes


def place(weight, pieces, hops):
    rows, cols = (lax.axis_size("tile"), lax.axis_size("fsdp"))
    tall = rows // 4
    share, width = pieces[0].shape[1:]
    t, f = (lax.axis_index("tile"), lax.axis_index("fsdp"))
    pieces = jnp.concatenate(pieces, axis=0)
    source_f = jnp.arange(cols)[:, None]
    source_t = jnp.arange(rows)[None, :]
    core = (source_t ^ t) & 1
    dx = ((source_t ^ t) >> 1) & 1
    dy = (t // 4 - source_t // 4) % tall
    order = [hops.index((0, hop)) for hop in range(1, cols)]
    hop = f ^ source_f
    at = jnp.array([0] + order)[hop]
    index = (core * 2 * tall + dy * 2 + dx) * (cols - 1) + at
    index = jnp.where(hop == 0, 0, index)
    whole = jnp.take(pieces, index.reshape(-1), axis=0).reshape(cols, rows * share, width)
    whole = lax.dynamic_update_index_in_dim(whole, weight, f, 0)
    return whole.reshape(-1, width)


def gelu(x):
    return 0.5 * x * (1.0 + lax.erf(x * (0.5**0.5)))


def one_hot(rows, width, target):
    n = lax.broadcasted_iota(jnp.int32, (rows, width), 0)
    return jnp.where(lax.broadcasted_iota(jnp.int32, (rows, width), 1) == target(n), 1.0, 0.0).astype(
        jnp.bfloat16
    )


def select(picker, values):
    return jnp.dot(picker, values, preferred_element_type=jnp.float32)


def put_borders(bundle, tile, half, chunk, edge):
    rows = edge // 2
    sides = one_hot(
        edge, rows * edge, lambda n: jnp.where(n < rows, n * edge, (n - rows) * edge + edge - 1)
    )
    sides = select(sides, chunk).astype(jnp.bfloat16)
    start = tile * 4 * edge
    bundle[pl.ds(start + 3 * edge + half * rows, rows), :] = sides[:rows]
    bundle[pl.ds(start + edge + half * rows, rows), :] = sides[rows:]
    if half == 0:
        bundle[pl.ds(start, edge), :] = chunk[:edge]
    else:
        bundle[pl.ds(start + 2 * edge, edge), :] = chunk[-edge:]


def request_of(links, tile, side, tiles, edge):
    near_id, near_side, flag = (links[i, tile, side] for i in range(3))
    home = lax.rem(near_id, tiles) * 4 + near_side
    turns = (1 if side >= 2 else 0) + jnp.where(near_side >= 2, 1, 0) + jnp.where(flag == 1, 0, 1)
    forward = lax.rem(turns, 2) == 0
    return home * edge + jnp.where(forward, 0, edge - 1), jnp.where(forward, 1, -1)


def put_corners(bundle, tiles, edge, asked=None):
    def source(n):
        corner = n & 3
        across = jnp.where((corner == 1) | (corner == 2), edge - 1, 0)
        return (n >> 2) * 4 * edge + jnp.where(corner >= 2, 2 * edge, 0) + across

    strips = tiles * 4 * edge
    cells = select(one_hot(PAD, strips, source), bundle[:strips, :])
    bundle[strips:, :] = cells.astype(jnp.bfloat16)
    if asked is not None:
        moved = select(one_hot(PAD, asked.shape[0], lambda n: n - tiles * 4), asked[...])
        below = lax.broadcasted_iota(jnp.int32, moved.shape, 0) >= tiles * 4
        bundle[strips:, :128] = jnp.where(below, moved, cells[:, :128]).astype(jnp.bfloat16)


def answer(out, bundle, asked, side, tiles, edge):
    strips = tiles * 4 * edge
    asked = asked.astype(jnp.float32)
    asked = jnp.concatenate([asked] * (strips // 128), axis=1)
    step = jnp.where(jnp.floor(asked * (1.0 / edge)) * edge == asked, 1.0, -1.0)
    n = lax.broadcasted_iota(jnp.int32, (edge, strips), 0).astype(jnp.float32)
    column = lax.broadcasted_iota(jnp.int32, (edge, strips), 1).astype(jnp.float32)
    for tile in range(tiles):
        row = tile * 4 + side
        picker = column == asked[row : row + 1] + step[row : row + 1] * n
        picker = jnp.where(picker, 1.0, 0.0).astype(jnp.bfloat16)
        out[tile * edge : (tile + 1) * edge, :] = select(picker, bundle[:strips, :]).astype(jnp.bfloat16)


def replies_kernel(tiles, edge, bundle, from_west, from_east, north, south, to_east, to_west):
    strips = tiles * 4 * edge
    for out, note, side in ((to_east, from_east, 3), (to_west, from_west, 1)):
        answer(out, bundle, note[0, :, note.shape[2] - 128 :], side, tiles, edge)
        out[tiles * edge : tiles * edge + PAD, :] = north[strips:, :]
        out[tiles * edge + PAD :, :] = south[strips:, :]


def replies(bundle, notes, north, south, tiles, edge):
    out = jax.ShapeDtypeStruct((tiles * edge + 2 * PAD, bundle.shape[1]), jnp.bfloat16)
    return pl.pallas_call(
        functools.partial(replies_kernel, tiles, edge),
        out_shape=(out, out),
        compiler_params=pltpu.CompilerParams(vmem_limit_bytes=8 << 20),
        name="replies",
    )(bundle, *notes, north, south)


def borders_kernel(asked, field, bundle):
    tiles, edge, _, channels = field.shape
    for tile in range(tiles):
        for half in range(2):
            rows = edge // 2
            chunk = field[tile, half * rows : (half + 1) * rows].reshape(rows * edge, channels)
            put_borders(bundle, tile, half, chunk, edge)
    put_corners(bundle, tiles, edge, asked)


def borders(field, asked):
    tiles, edge, _, channels = field.shape
    return pl.pallas_call(
        borders_kernel,
        out_shape=jax.ShapeDtypeStruct((tiles * 4 * edge + PAD, channels), jnp.bfloat16),
        compiler_params=pltpu.CompilerParams(vmem_limit_bytes=16 << 20),
        name="borders",
    )(asked, field)


def surround(field, near, side_links, corner_links, chosen, halos, wide):
    tiles, edge, _, channels = field.shape
    strips = tiles * 4 * edge
    column = lax.broadcasted_iota(jnp.int32, (edge, channels), 0)

    def put(tile, row, middle, before, after):
        spread = middle.astype(jnp.float32)
        left = jnp.where(column == 0, before, pltpu.roll(spread, 1, 0))
        right = jnp.where(column == edge - 1, after, pltpu.roll(spread, edge - 1, 0))
        wide[tile, row, :, :channels] = left.astype(jnp.bfloat16)
        wide[tile, row, :, channels : 2 * channels] = middle.astype(jnp.bfloat16)
        wide[tile, row, :, 2 * channels :] = right.astype(jnp.bfloat16)

    for tile in range(tiles):
        for side in range(4):
            if chosen[side]:
                halos[tile, side] = near[side][tile * edge : (tile + 1) * edge, :].astype(jnp.float32)
                continue
            first, step = request_of(side_links, tile, side, tiles, edge)
            picker = one_hot(edge, strips, lambda n: first + step * n)
            halos[tile, side] = select(picker, near[side][:strips, :])
        cells = []
        for corner, (source, low) in enumerate(((3, 0), (1, 0), (1, PAD), (3, PAD))):
            near_id, near_corner, flag = (corner_links[i, tile, corner] for i in range(3))
            pick = jnp.where(flag == 1, lax.rem(near_id, tiles) * 4 + near_corner, -1)
            picker = one_hot(8, PAD, lambda n: pick)
            cells_at = tiles * edge if chosen[source] else strips + PAD
            cells.append(select(picker, near[source][cells_at + low : cells_at + low + PAD, :])[:1])
        put(tile, 0, halos[tile, 0], cells[0], cells[1])
        put(tile, edge + 1, halos[tile, 2], cells[3], cells[2])

        @pl.loop(0, edge // 4)
        def _(block):
            for offset in range(4):
                row = block * 4 + offset
                before = halos[tile, 3, pl.ds(row, 1), :]
                after = halos[tile, 1, pl.ds(row, 1), :]
                put(tile, row + 1, field[tile, row], before, after)


def fetch_weight(sources, places, hops, whole, place_of):
    own, *pieces = sources
    share = pieces[0].shape[1]
    cols = len(hops) + 1
    width = whole.shape[1]
    rows = own.shape[0] // share
    t, f = (place_of[0], place_of[1])
    tall = rows // 4
    whole[pl.ds(pl.multiple_of(f * rows * share, share), rows * share), :] = own[...]
    for piece, (core, step, low) in zip(pieces, places):
        dy, dx = divmod(step, 2)
        far_y = lax.rem(t // 4 + tall - dy, tall)
        far_x = lax.rem(t // 2 + dx, 2)
        far = far_y * 4 + far_x * 2 + lax.rem(t + core, 2)
        high = min(low + piece.shape[2], width)
        for i, (back, flip) in enumerate(hops):
            far_f = lax.rem(f + cols + back, cols) ^ flip
            start = pl.multiple_of((far_f * rows + far) * share, share)
            whole[pl.ds(start, share), low:high] = piece[i, :, : high - low]


def conv_kernel(places, hops, chosen, pooling, *refs):
    place_of, side_links, corner_links, field, north, east, south, west, bias = refs[:9]
    near = (north, east, south, west)
    count = 1 + len(places)
    sources = refs[9 : 9 + count]
    asking = 2 if chosen[1] and not pooling else 0
    notes = refs[9 + count : 9 + count + asking]
    outs = refs[9 + count + asking : -5]
    halos, wide, whole, total, bundle = refs[-5:]
    tiles, edge, _, channels = field.shape
    if count == 1:
        whole = sources[0]
    else:
        fetch_weight(sources, places, hops, whole, place_of)
    surround(field, near, side_links, corner_links, chosen, halos, wide)
    rows = edge // 2
    depth = 3 * channels
    for tile in range(tiles):
        for half in range(2):
            low = half * rows
            summed = bias[...]
            for tap in range(3):
                window = wide[tile, low + tap : low + tap + rows].reshape(rows * edge, depth)
                summed = summed + lax.dot_general(
                    window,
                    whole[:, tap * depth : (tap + 1) * depth],
                    (((1,), (1,)), ((), ())),
                    preferred_element_type=jnp.float32,
                )
            act = gelu(summed)
            if pooling:
                width = act.shape[1]
                act = act.reshape(rows // 2, 2, edge, width)
                act = (act[:, 0] + act[:, 1]).reshape(rows // 2 * edge, width)
                mean = []
                for lanes in range(0, width, 128):
                    total[...] = act[:, lanes : lanes + 128]
                    even = total[pl.ds(0, rows * edge // 4, stride=2), :]
                    odd = total[pl.ds(1, rows * edge // 4, stride=2), :]
                    mean.append(((even + odd) * 0.25).astype(jnp.bfloat16))
                mean = jnp.concatenate(mean, axis=1)
                outs[0][tile, low // 2 : (low + rows) // 2] = mean.reshape(rows // 2, edge // 2, width)
            else:
                hidden = act.astype(jnp.bfloat16)
                outs[0][tile, low : low + rows] = hidden.reshape(rows, edge, act.shape[1])
                put_borders(bundle, tile, half, hidden, edge)
    if not pooling:
        put_corners(bundle, tiles, edge)
        for side, out in enumerate(outs[1:]):
            if notes and side % 2:
                note = notes[(3 - side) // 2]
                asked = note[0, :, note.shape[2] - 128 :]
            else:
                asked = near[side][tiles * 4 * edge + tiles * 4 : tiles * 4 * edge + PAD, :128]
            answer(out, bundle, asked, (side + 2) % 4, tiles, edge)
            if side in (0, 2):
                out[tiles * edge :, :] = bundle[tiles * 4 * edge :, :]


def conv(field, near, links, bias, weight, chosen, pooling, notes=()):
    sources, places, hops = weight
    tiles, edge, _, channels = field.shape
    width = bias.shape[0]
    if pooling:
        outs = (jax.ShapeDtypeStruct((tiles, edge // 2, edge // 2, width), jnp.bfloat16),)
    else:
        outs = (jax.ShapeDtypeStruct((tiles, edge, edge, width), jnp.bfloat16),) + tuple(
            jax.ShapeDtypeStruct((tiles * edge + extra, width), jnp.bfloat16) for extra in (PAD, 0, PAD, 0)
        )
    vmem = pl.BlockSpec(memory_space=pltpu.VMEM)
    smem = pl.BlockSpec(memory_space=pltpu.SMEM)
    flops = 2 * tiles * edge * edge * 9 * channels * width
    return pl.pallas_call(
        functools.partial(conv_kernel, places, hops, chosen, pooling),
        out_shape=outs,
        in_specs=[smem] * 3 + [vmem] * (6 + len(sources) + len(notes)),
        out_specs=[vmem] * len(outs),
        scratch_shapes=[
            pltpu.VMEM((tiles, 4, edge, channels), jnp.float32),
            pltpu.VMEM((tiles, edge + 2, edge, 3 * channels), jnp.bfloat16),
            pltpu.VMEM((width if len(sources) > 1 else 8, 9 * channels), jnp.bfloat16),
            pltpu.VMEM((edge * edge // 4, 128), jnp.float32),
            pltpu.VMEM((tiles * 4 * edge + PAD, width), jnp.bfloat16),
        ],
        cost_estimate=pl.CostEstimate(flops=flops, bytes_accessed=8 << 20, transcendentals=0),
        compiler_params=pltpu.CompilerParams(vmem_limit_bytes=GRANT),
        name="second" if pooling else "first",
    )(
        *links,
        field,
        *near,
        bias.reshape(1, width),
        *sources,
        *notes,
    )


def exchange(to_north, to_east, to_south, to_west):
    north = shift(to_south, 1, 0)
    south = shift(to_north, -1, 0)
    cells = [north[-PAD:], south[-PAD:]]
    west = shift(jnp.concatenate([to_east, *cells], axis=0), 0, 1)
    east = shift(jnp.concatenate([to_west, *cells], axis=0), 0, -1)
    return north, east, south, west


def codes(side_links, share, edge):
    tiles = side_links.shape[0]
    near_id, near_side, flag = (side_links[..., i] for i in range(3))
    turned = (jnp.arange(4) >= 2)[None, :]
    forward = ~(turned ^ (near_side >= 2) ^ (flag != 1))
    first = (near_id % tiles * 4 + near_side) * edge + jnp.where(forward, 0, edge - 1)
    first = jnp.concatenate([first.reshape(-1), jnp.zeros((share - tiles * 4,), first.dtype)])
    return jnp.broadcast_to(first.astype(jnp.bfloat16)[:, None], (share, 128))


def sources_of(weight, relay, asked):
    pieces, places, hops, notes = gather_rows(weight, relay, asked)
    if pieces[0].shape[1] % 16 == 0:
        return ((weight, *pieces), tuple(places), tuple(hops)), notes
    return ((place(weight, pieces, hops),), (), ()), notes


def shards(
    tiles_in, first_weight, first_bias, second_weight, second_bias, side_links, corner_links
):
    tiles, edge, _, _ = tiles_in.shape
    small = lax.axis_size("tile") == 8
    place_of = jnp.stack([lax.axis_index("tile"), lax.axis_index("fsdp")])
    asked = codes(side_links, PAD, edge)
    side_links = side_links.transpose(2, 0, 1)
    links = (place_of, side_links, corner_links.transpose(2, 0, 1))
    first, notes = sources_of(first_weight, False, asked if small else None)
    second, _ = sources_of(second_weight, small, None)
    bundle = borders(tiles_in, asked)
    if notes:
        north = shift(bundle, 1, 0)
        south = shift(bundle, -1, 0)
        to_east, to_west = replies(bundle, notes, north, south, tiles, edge)
        near = (north, shift(to_west, 0, -1), south, shift(to_east, 0, 1))
        chosen = (False, True, False, True)
    else:
        near = exchange(bundle, bundle, bundle, bundle)
        chosen = (False,) * 4
    hidden, *strips = conv(
        tiles_in, near, links, first_bias, first, chosen, False, notes or ()
    )
    near = exchange(*strips)
    return conv(hidden, near, links, second_bias, second, (True,) * 4, True)[0]


def solution(mesh):
    placed = (
        P(AXES, None, None, None),
        P("fsdp", None),
        P(),
        P("fsdp", None),
        P(),
        P(AXES, None, None),
        P(AXES, None, None),
    )
    return jax.shard_map(
        shards,
        mesh=mesh,
        in_specs=placed,
        out_specs=P(AXES, None, None, None),
        check_vma=False,
    )
```

```python
import functools

import jax
import jax.numpy as jnp
from jax import lax
from jax.experimental import pallas as pl
from jax.experimental.pallas import tpu as pltpu
from jax.sharding import PartitionSpec as P


AXES = ("tile", "fsdp")
PAD = 16
GRANT = 36 << 20


def move(x, target):
    rows, cols = (lax.axis_size("tile"), lax.axis_size("fsdp"))
    pairs = []
    for t in range(rows):
        for f in range(cols):
            there_t, there_f = target(t, f)
            pairs.append((t * cols + f, (there_t % rows) * cols + there_f % cols))
    return lax.ppermute(x, AXES, pairs)


def shift(x, rows, cols):
    return move(x, lambda t, f: (t + rows, f + cols))


def doublings(cols):
    bits = [1 << k for k in range(cols.bit_length() - 1)]
    return bits[::-1]


def across(x, dy, dx):
    tall = lax.axis_size("tile") // 4
    return move(x, lambda t, f: (((t // 4 + dy) % tall) * 4 + ((t // 2 % 2) ^ dx) * 2 + t % 2, f))


def gather_rows(weight, relay, asked):
    rows, cols = (lax.axis_size("tile"), lax.axis_size("fsdp"))
    tall = rows // 4
    share = weight.shape[0] // rows
    width = weight.shape[1]
    parts = weight.reshape(rows, share, width)
    mine = lax.dynamic_index_in_dim(parts, lax.axis_index("tile"), 0, keepdims=True)
    notes = None
    if asked is not None:
        mine = jnp.concatenate([mine, asked[None]], axis=2)
        parts = [shift(mine, 0, k) for k in range(1, cols)]
        hops = [(-k, 0) for k in range(1, cols)]
        notes = (parts[0], parts[-1])
    elif relay and cols == 4:
        far = move(mine, lambda t, f: (t, f ^ 2))
        by = move(mine, lambda t, f: (t, f ^ 1))
        parts = [far, by, move(far, lambda t, f: (t, f ^ 1))]
        hops = [(0, 2), (0, 1), (0, 3)]
    else:
        parts, hops = ([mine], [(0, 0)])
        for bit in doublings(cols):
            there = parts[0] if len(parts) == 1 else jnp.concatenate(parts, axis=0)
            parts.append(move(there, lambda t, f: (t, f ^ bit)))
            hops += [(0, hop ^ bit) for _, hop in hops]
        parts, hops = (parts[1:], hops[1:])
    unit = jnp.concatenate(parts, axis=0)
    sent = [(unit, 0, 0)]
    for step in range(1, 2 * tall):
        if not (relay and step == 3):
            sent.append((across(unit, *divmod(step, 2)), step, 0))
    if relay:
        half = width // 2
        by_x, by_y = (sent[1][0], sent[2][0])
        sent.append((across(by_x[:, :, :half], 1, 0), 3, 0))
        sent.append((across(by_y[:, :, half:], 0, 1), 3, half))
    other = [move(x, lambda t, f: (t ^ 1, f)) for x, _, _ in sent]
    places = [(0, *place[1:]) for place in sent] + [(1, *place[1:]) for place in sent]
    return [x for x, _, _ in sent] + other, places, hops, notes


def place(weight, pieces, hops):
    rows, cols = (lax.axis_size("tile"), lax.axis_size("fsdp"))
    tall = rows // 4
    share, width = pieces[0].shape[1:]
    t, f = (lax.axis_index("tile"), lax.axis_index("fsdp"))
    pieces = jnp.concatenate(pieces, axis=0)
    source_f = jnp.arange(cols)[:, None]
    source_t = jnp.arange(rows)[None, :]
    core = (source_t ^ t) & 1
    dx = ((source_t ^ t) >> 1) & 1
    dy = (t // 4 - source_t // 4) % tall
    order = [hops.index((0, hop)) for hop in range(1, cols)]
    hop = f ^ source_f
    at = jnp.array([0] + order)[hop]
    index = (core * 2 * tall + dy * 2 + dx) * (cols - 1) + at
    index = jnp.where(hop == 0, 0, index)
    whole = jnp.take(pieces, index.reshape(-1), axis=0).reshape(cols, rows * share, width)
    whole = lax.dynamic_update_index_in_dim(whole, weight, f, 0)
    return whole.reshape(-1, width)


def gelu(x):
    return 0.5 * x * (1.0 + lax.erf(x * (0.5**0.5)))


def one_hot(rows, width, target):
    n = lax.broadcasted_iota(jnp.int32, (rows, width), 0)
    return jnp.where(lax.broadcasted_iota(jnp.int32, (rows, width), 1) == target(n), 1.0, 0.0).astype(
        jnp.bfloat16
    )


def select(picker, values):
    return jnp.dot(picker, values, preferred_element_type=jnp.float32)


def put_borders(bundle, tile, half, chunk, edge):
    rows = edge // 2
    sides = one_hot(
        edge, rows * edge, lambda n: jnp.where(n < rows, n * edge, (n - rows) * edge + edge - 1)
    )
    sides = select(sides, chunk).astype(jnp.bfloat16)
    start = tile * 4 * edge
    bundle[pl.ds(start + 3 * edge + half * rows, rows), :] = sides[:rows]
    bundle[pl.ds(start + edge + half * rows, rows), :] = sides[rows:]
    if half == 0:
        bundle[pl.ds(start, edge), :] = chunk[:edge]
    else:
        bundle[pl.ds(start + 2 * edge, edge), :] = chunk[-edge:]


def request_of(links, tile, side, tiles, edge):
    near_id, near_side, flag = (links[i, tile, side] for i in range(3))
    home = lax.rem(near_id, tiles) * 4 + near_side
    turns = (1 if side >= 2 else 0) + jnp.where(near_side >= 2, 1, 0) + jnp.where(flag == 1, 0, 1)
    forward = lax.rem(turns, 2) == 0
    return home * edge + jnp.where(forward, 0, edge - 1), jnp.where(forward, 1, -1)


def put_corners(bundle, tiles, edge, asked=None):
    def source(n):
        corner = n & 3
        across = jnp.where((corner == 1) | (corner == 2), edge - 1, 0)
        return (n >> 2) * 4 * edge + jnp.where(corner >= 2, 2 * edge, 0) + across

    strips = tiles * 4 * edge
    cells = select(one_hot(PAD, strips, source), bundle[:strips, :])
    bundle[strips:, :] = cells.astype(jnp.bfloat16)
    if asked is not None:
        moved = select(one_hot(PAD, asked.shape[0], lambda n: n - tiles * 4), asked[...])
        below = lax.broadcasted_iota(jnp.int32, moved.shape, 0) >= tiles * 4
        bundle[strips:, :128] = jnp.where(below, moved, cells[:, :128]).astype(jnp.bfloat16)


def answer(out, bundle, asked, side, tiles, edge):
    strips = tiles * 4 * edge
    asked = asked.astype(jnp.float32)
    asked = jnp.concatenate([asked] * (strips // 128), axis=1)
    step = jnp.where(jnp.floor(asked * (1.0 / edge)) * edge == asked, 1.0, -1.0)
    n = lax.broadcasted_iota(jnp.int32, (edge, strips), 0).astype(jnp.float32)
    column = lax.broadcasted_iota(jnp.int32, (edge, strips), 1).astype(jnp.float32)
    for tile in range(tiles):
        row = tile * 4 + side
        picker = column == asked[row : row + 1] + step[row : row + 1] * n
        picker = jnp.where(picker, 1.0, 0.0).astype(jnp.bfloat16)
        out[tile * edge : (tile + 1) * edge, :] = select(picker, bundle[:strips, :]).astype(jnp.bfloat16)


def replies_kernel(tiles, edge, bundle, from_west, from_east, north, south, to_east, to_west):
    strips = tiles * 4 * edge
    for out, note, side in ((to_east, from_east, 3), (to_west, from_west, 1)):
        answer(out, bundle, note[0, :, note.shape[2] - 128 :], side, tiles, edge)
        out[tiles * edge : tiles * edge + PAD, :] = north[strips:, :]
        out[tiles * edge + PAD :, :] = south[strips:, :]


def replies(bundle, notes, north, south, tiles, edge):
    out = jax.ShapeDtypeStruct((tiles * edge + 2 * PAD, bundle.shape[1]), jnp.bfloat16)
    return pl.pallas_call(
        functools.partial(replies_kernel, tiles, edge),
        out_shape=(out, out),
        compiler_params=pltpu.CompilerParams(vmem_limit_bytes=8 << 20),
        name="replies",
    )(bundle, *notes, north, south)


def borders_kernel(asked, field, bundle):
    tiles, edge, _, channels = field.shape
    for tile in range(tiles):
        for half in range(2):
            rows = edge // 2
            chunk = field[tile, half * rows : (half + 1) * rows].reshape(rows * edge, channels)
            put_borders(bundle, tile, half, chunk, edge)
    put_corners(bundle, tiles, edge, asked)


def borders(field, asked):
    tiles, edge, _, channels = field.shape
    return pl.pallas_call(
        borders_kernel,
        out_shape=jax.ShapeDtypeStruct((tiles * 4 * edge + PAD, channels), jnp.bfloat16),
        compiler_params=pltpu.CompilerParams(vmem_limit_bytes=16 << 20),
        name="borders",
    )(asked, field)


def surround(field, near, side_links, corner_links, chosen, halos, wide):
    tiles, edge, _, channels = field.shape
    strips = tiles * 4 * edge
    column = lax.broadcasted_iota(jnp.int32, (edge, channels), 0)

    def put(tile, row, middle, before, after):
        spread = middle.astype(jnp.float32)
        left = jnp.where(column == 0, before, pltpu.roll(spread, 1, 0))
        right = jnp.where(column == edge - 1, after, pltpu.roll(spread, edge - 1, 0))
        wide[tile, row, :, :channels] = left.astype(jnp.bfloat16)
        wide[tile, row, :, channels : 2 * channels] = middle.astype(jnp.bfloat16)
        wide[tile, row, :, 2 * channels :] = right.astype(jnp.bfloat16)

    for tile in range(tiles):
        for side in range(4):
            if chosen[side]:
                halos[tile, side] = near[side][tile * edge : (tile + 1) * edge, :].astype(jnp.float32)
                continue
            first, step = request_of(side_links, tile, side, tiles, edge)
            picker = one_hot(edge, strips, lambda n: first + step * n)
            halos[tile, side] = select(picker, near[side][:strips, :])
        cells = []
        for corner, (source, low) in enumerate(((3, 0), (1, 0), (1, PAD), (3, PAD))):
            near_id, near_corner, flag = (corner_links[i, tile, corner] for i in range(3))
            pick = lax.rem(near_id, tiles) * 4 + near_corner
            if all(chosen):
                pick, low = (pick + (0 if low else PAD // 2), 0)
            pick = jnp.where(flag == 1, pick, -1)
            picker = one_hot(8, PAD, lambda n: pick)
            cells_at = tiles * edge if chosen[source] else strips + PAD
            cells.append(select(picker, near[source][cells_at + low : cells_at + low + PAD, :])[:1])
        put(tile, 0, halos[tile, 0], cells[0], cells[1])
        put(tile, edge + 1, halos[tile, 2], cells[3], cells[2])

        @pl.loop(0, edge // 4)
        def _(block):
            for offset in range(4):
                row = block * 4 + offset
                before = halos[tile, 3, pl.ds(row, 1), :]
                after = halos[tile, 1, pl.ds(row, 1), :]
                put(tile, row + 1, field[tile, row], before, after)


def fetch_weight(sources, places, hops, whole, place_of):
    own, *pieces = sources
    share = pieces[0].shape[1]
    cols = len(hops) + 1
    width = whole.shape[1]
    rows = own.shape[0] // share
    t, f = (place_of[0], place_of[1])
    tall = rows // 4
    whole[pl.ds(pl.multiple_of(f * rows * share, share), rows * share), :] = own[...]
    for piece, (core, step, low) in zip(pieces, places):
        dy, dx = divmod(step, 2)
        far_y = lax.rem(t // 4 + tall - dy, tall)
        far_x = lax.rem(t // 2 + dx, 2)
        far = far_y * 4 + far_x * 2 + lax.rem(t + core, 2)
        high = min(low + piece.shape[2], width)
        for i, (back, flip) in enumerate(hops):
            far_f = lax.rem(f + cols + back, cols) ^ flip
            start = pl.multiple_of((far_f * rows + far) * share, share)
            whole[pl.ds(start, share), low:high] = piece[i, :, : high - low]


def conv_kernel(places, hops, chosen, pooling, *refs):
    place_of, side_links, corner_links, field, north, east, south, west, bias = refs[:9]
    near = (north, east, south, west)
    count = 1 + len(places)
    sources = refs[9 : 9 + count]
    asking = 2 if chosen[1] and not pooling else 0
    notes = refs[9 + count : 9 + count + asking]
    outs = refs[9 + count + asking : -5]
    halos, wide, whole, total, bundle = refs[-5:]
    tiles, edge, _, channels = field.shape
    if count == 1:
        whole = sources[0]
    else:
        fetch_weight(sources, places, hops, whole, place_of)
    surround(field, near, side_links, corner_links, chosen, halos, wide)
    rows = edge // 2
    depth = 3 * channels
    for tile in range(tiles):
        for half in range(2):
            low = half * rows
            summed = bias[...]
            for tap in range(3):
                window = wide[tile, low + tap : low + tap + rows].reshape(rows * edge, depth)
                summed = summed + lax.dot_general(
                    window,
                    whole[:, tap * depth : (tap + 1) * depth],
                    (((1,), (1,)), ((), ())),
                    preferred_element_type=jnp.float32,
                )
            act = gelu(summed)
            if pooling:
                width = act.shape[1]
                act = act.reshape(rows // 2, 2, edge, width)
                act = (act[:, 0] + act[:, 1]).reshape(rows // 2 * edge, width)
                mean = []
                for lanes in range(0, width, 128):
                    total[...] = act[:, lanes : lanes + 128]
                    even = total[pl.ds(0, rows * edge // 4, stride=2), :]
                    odd = total[pl.ds(1, rows * edge // 4, stride=2), :]
                    mean.append(((even + odd) * 0.25).astype(jnp.bfloat16))
                mean = jnp.concatenate(mean, axis=1)
                outs[0][tile, low // 2 : (low + rows) // 2] = mean.reshape(rows // 2, edge // 2, width)
            else:
                hidden = act.astype(jnp.bfloat16)
                outs[0][tile, low : low + rows] = hidden.reshape(rows, edge, act.shape[1])
                put_borders(bundle, tile, half, hidden, edge)
    if not pooling:
        put_corners(bundle, tiles, edge)
        for side, out in enumerate(outs[1:]):
            if notes and side % 2:
                note = notes[(3 - side) // 2]
                asked = note[0, :, note.shape[2] - 128 :]
            else:
                asked = near[side][tiles * 4 * edge + tiles * 4 : tiles * 4 * edge + PAD, :128]
            answer(out, bundle, asked, (side + 2) % 4, tiles, edge)
            cells = bundle[tiles * 4 * edge :, :]
            if side == 0:
                out[tiles * edge :, :] = cells
            if side == 2:
                lower = one_hot(PAD, PAD, lambda n: n - PAD // 2)
                out[tiles * edge :, :] = select(lower, cells).astype(jnp.bfloat16)


def conv(field, near, links, bias, weight, chosen, pooling, notes=()):
    sources, places, hops = weight
    tiles, edge, _, channels = field.shape
    width = bias.shape[0]
    if pooling:
        outs = (jax.ShapeDtypeStruct((tiles, edge // 2, edge // 2, width), jnp.bfloat16),)
    else:
        outs = (jax.ShapeDtypeStruct((tiles, edge, edge, width), jnp.bfloat16),) + tuple(
            jax.ShapeDtypeStruct((tiles * edge + extra, width), jnp.bfloat16) for extra in (PAD, 0, PAD, 0)
        )
    vmem = pl.BlockSpec(memory_space=pltpu.VMEM)
    smem = pl.BlockSpec(memory_space=pltpu.SMEM)
    flops = 2 * tiles * edge * edge * 9 * channels * width
    return pl.pallas_call(
        functools.partial(conv_kernel, places, hops, chosen, pooling),
        out_shape=outs,
        in_specs=[smem] * 3 + [vmem] * (6 + len(sources) + len(notes)),
        out_specs=[vmem] * len(outs),
        scratch_shapes=[
            pltpu.VMEM((tiles, 4, edge, channels), jnp.float32),
            pltpu.VMEM((tiles, edge + 2, edge, 3 * channels), jnp.bfloat16),
            pltpu.VMEM((width if len(sources) > 1 else 8, 9 * channels), jnp.bfloat16),
            pltpu.VMEM((edge * edge // 4, 128), jnp.float32),
            pltpu.VMEM((tiles * 4 * edge + PAD, width), jnp.bfloat16),
        ],
        cost_estimate=pl.CostEstimate(flops=flops, bytes_accessed=8 << 20, transcendentals=0),
        compiler_params=pltpu.CompilerParams(vmem_limit_bytes=GRANT),
        name="second" if pooling else "first",
    )(
        *links,
        field,
        *near,
        bias.reshape(1, width),
        *sources,
        *notes,
    )


def exchange(to_north, to_east, to_south, to_west, name):
    north = shift(to_south, 1, 0)
    south = shift(to_north, -1, 0)
    if name == "g":
        cells = [north[-PAD:] + south[-PAD:]]
    else:
        cells = [north[-PAD:], south[-PAD:]]
    west = shift(jnp.concatenate([to_east, *cells], axis=0), 0, 1)
    east = shift(jnp.concatenate([to_west, *cells], axis=0), 0, -1)
    return north, east, south, west


def codes(side_links, share, edge):
    tiles = side_links.shape[0]
    near_id, near_side, flag = (side_links[..., i] for i in range(3))
    turned = (jnp.arange(4) >= 2)[None, :]
    forward = ~(turned ^ (near_side >= 2) ^ (flag != 1))
    first = (near_id % tiles * 4 + near_side) * edge + jnp.where(forward, 0, edge - 1)
    first = jnp.concatenate([first.reshape(-1), jnp.zeros((share - tiles * 4,), first.dtype)])
    return jnp.broadcast_to(first.astype(jnp.bfloat16)[:, None], (share, 128))


def sources_of(weight, relay, asked):
    pieces, places, hops, notes = gather_rows(weight, relay, asked)
    if pieces[0].shape[1] % 16 == 0:
        return ((weight, *pieces), tuple(places), tuple(hops)), notes
    return ((place(weight, pieces, hops),), (), ()), notes


def shards(
    tiles_in, first_weight, first_bias, second_weight, second_bias, side_links, corner_links
):
    tiles, edge, _, _ = tiles_in.shape
    small = lax.axis_size("tile") == 8
    place_of = jnp.stack([lax.axis_index("tile"), lax.axis_index("fsdp")])
    asked = codes(side_links, PAD, edge)
    side_links = side_links.transpose(2, 0, 1)
    links = (place_of, side_links, corner_links.transpose(2, 0, 1))
    first, notes = sources_of(first_weight, False, asked if small else None)
    second, _ = sources_of(second_weight, small, None)
    bundle = borders(tiles_in, asked)
    if notes:
        north = shift(bundle, 1, 0)
        south = shift(bundle, -1, 0)
        to_east, to_west = replies(bundle, notes, north, south, tiles, edge)
        near = (north, shift(to_west, 0, -1), south, shift(to_east, 0, 1))
        chosen = (False, True, False, True)
    else:
        near = exchange(bundle, bundle, bundle, bundle, "h")
        chosen = (False,) * 4
    hidden, *strips = conv(
        tiles_in, near, links, first_bias, first, chosen, False, notes or ()
    )
    near = exchange(*strips, "g")
    return conv(hidden, near, links, second_bias, second, (True,) * 4, True)[0]


def solution(mesh):
    placed = (
        P(AXES, None, None, None),
        P("fsdp", None),
        P(),
        P("fsdp", None),
        P(),
        P(AXES, None, None),
        P(AXES, None, None),
    )
    return jax.shard_map(
        shards,
        mesh=mesh,
        in_specs=placed,
        out_specs=P(AXES, None, None, None),
        check_vma=False,
    )
```
